256 devices in a mesh: level: 2 (over core), group: 32 (over y, z), leaf: 4 (over x).
Axes of the slice: x: 4, y: 4, z: 8, core: 2. Of those that a mesh axis runs over, the one named last changes fastest.
Arguments:
- queries: bfloat16 [3072, 2048], P('group'), may hold values from -6 to 6
- weights: bfloat16 [2, 4, 32, 2048, 1024], P('level', 'leaf', 'group'), may hold values from -0.125 to 0.125
- block_mask: int32 [2, 4, 32, 16], P('level', 'leaf', 'group'), may hold values 0 or 1
- label_map: int32 [2, 4, 32, 1024], P('level', 'leaf', 'group'), may hold values from 0 to 1023, each once within a row
- beam_lists: int32 [2, 3072, 4], P('level', 'group'), may hold values from 0 to 31, all different within a row; in each aligned block of 32 rows (0 to 31, 32 to 63, ..., all dimensions but the last counted through in order) at most 8 rows name the same one
- root_score: bfloat16 [3072, 4], P('group'), may hold values from 0.19921875 to 1
- parent_pos: int32 [3072, 4], P('group'), may hold values from 0 to 4095
Outputs:
- scores: float32 [2, 3072, 4, 1024], P('level', 'group', None, 'leaf')
The draws below stay inside these ranges and needn't reach their ends.
Inputs may be any that keep to these rules, and one draw needn't show every extreme that they name: `beam_lists`: each row names 4 different groups; in each aligned block of 32 rows (both levels' rows taken in order) no group is named by more than 8 rows, a bound that some block reaches. `label_map`: each row is a permutation of 0 to 1023.
All inputs are finite; a program needn't handle non-finite values. No bound on the sum of `block_mask` on one device may be relied on, other than what follows from the above.
Results may differ from the reference program's by a relative error of at most 0.0013.
Values may be sent and summed in bfloat16 or wider, within the bound.
A program may use at most 128 MiB of HBM per device.

```python
import math
import jax
import jax.numpy as jnp
import numpy as np
from jax import lax

D = 2048
L = 1024
B = 4
QBLK = 32
MASKB = 16
GROUPS = 32
CAP = 8
TREES = 4
QUERIES = 3072


def touch_ends(array, key, least, largest):
    extent = array.shape
    index_at = [jax.random.randint(jax.random.fold_in(key, axis), (), 0, extent[axis]) for axis in range(len(extent))]
    array = array.at[tuple(index_at)].set(least)
    longest = extent.index(max(extent))
    index_at[longest] = (index_at[longest] + 1) % extent[longest]
    return array.at[tuple(index_at)].set(largest)


def block_levels(own_key, extent, shards, low, largest):
    level = 1.0
    for position, parts in shards:
        steps = jax.random.uniform(jax.random.fold_in(jax.random.fold_in(own_key, 6), position), (parts,), jnp.float32, low / len(shards), largest / len(shards))
        level = level * jnp.repeat(jnp.exp(steps), extent[position] // parts).reshape((-1,) + (1,) * (len(extent) - 1 - position))
    return level


def shared_out(own_key, own, number, rows, number_of, top, limit, lean):
    order = jax.random.permutation(own_key, number_of)
    heavy_load, usual = shares(number_of, rows * top, limit, lean, True), shares(number_of, rows * top, limit, lean, False)
    places = jnp.arange(number_of)

    def named(lengths, rotation):
        used = int((lengths > 0).sum())
        fixed = max(1, used // 4)
        moved = fixed + (places - fixed + rotation * (used - fixed)) % max(1, number_of - fixed)
        return jnp.zeros((number_of,), jnp.int32).at[order[jnp.where(places < fixed, places, moved)]].set(jnp.asarray(lengths, jnp.int32))

    lengths = jnp.where(number % 4 == 0, named(heavy_load, number // 4), named(usual, number - number // 4 - 1))
    mixed = jax.random.permutation(jax.random.fold_in(own, 3), number_of)
    giver, receiver = mixed[0:number_of // 2 * 2:2], mixed[1:number_of // 2 * 2:2]
    margin = jnp.minimum(lengths[giver] - 1, limit - lengths[receiver]) // 2
    margin = jnp.where((giver == order[0]) | (receiver == order[0]) | (lengths[receiver] == 0), 0, jnp.maximum(margin, 0))
    moved = jax.random.randint(jax.random.fold_in(own, 4), (number_of // 2,), 0, 1 << 20) % (margin + 1)
    lengths = lengths.at[giver].add(-moved).at[receiver].add(moved)
    labels = jnp.searchsorted(jnp.cumsum(lengths), jnp.arange(rows * top), side="right").astype(jnp.int32)
    table = labels.reshape(top, rows).T
    table = table[jax.random.permutation(jax.random.fold_in(own, 1), rows)]
    rotation = jax.random.randint(jax.random.fold_in(own, 2), (rows, 1), 0, top)
    return jnp.take_along_axis(table, (jnp.arange(top)[None, :] + rotation) % top, axis=1)


def shares(number_of, total, bound, slope, full):
    portions = [(1 << 20) // math.isqrt(grade ** slope) + 1 for grade in range(1, number_of + 1)]
    largest = bound if full else min(bound, max(-(-total // number_of), total * portions[0] // sum(portions)))
    least = 1 if total - largest >= number_of - 1 else 0
    holding, spare = [largest] + [least] * (number_of - 1), total - largest - least * (number_of - 1)
    while spare > 0:
        movable = [i for i in range(1, number_of) if holding[i] < largest] or [i for i in range(1, number_of) if holding[i] < bound]
        pool, remaining = sum([portions[i] for i in movable]), spare
        for i in movable:
            extra = min(bound - holding[i], max(1, remaining * portions[i] // pool), spare)
            holding[i] = holding[i] + extra
            spare = spare - extra
    return np.array(holding)


def centred(own_key, shape, scale, reach, split=(), held_as=jnp.bfloat16):
    factor_of = block_levels(own_key, shape, split, -0.22, 0.18) if split else 1.0
    values = jax.random.normal(own_key, shape, jnp.float32) * scale * factor_of
    return jnp.minimum(jnp.maximum(values, -reach), reach).astype(held_as)


def setup_inputs(seed: int = 0) -> dict:
    seeds = jax.random.split(jax.random.key(seed), 8)
    queries = centred(seeds[0], (QUERIES, D), 1.0, 6.0, ((0, 32),))
    weights = centred(seeds[1], (2, TREES, GROUPS, D, L), D ** -0.5, 0.125, ((0, 2), (1, 4), (2, 32)))
    block_mask = touch_ends((jax.random.randint(seeds[2], (2, TREES, GROUPS, MASKB), 0, 4) < 3).astype(jnp.int32), jax.random.fold_in(seeds[2], 1), 0, 1)
    label_map = jax.vmap(lambda own: jax.random.permutation(own, L))(jax.random.split(seeds[3], 2 * TREES * GROUPS)).reshape((2, TREES, GROUPS, L)).astype(jnp.int32)
    beam_lists_keys = jax.random.split(jax.random.fold_in(seeds[4], 1), 2 * QUERIES // QBLK)
    beam_lists_turns = jax.random.permutation(jax.random.fold_in(seeds[4], 3), 2 * QUERIES // QBLK)
    beam_lists = jax.vmap(lambda own, number: shared_out(jax.random.fold_in(seeds[4], 2), own, number, QBLK, GROUPS, B, CAP, 2))(beam_lists_keys, beam_lists_turns).reshape((2, QUERIES, B))
    root_score = jnp.clip(0.19921875 + 0.80078125 * jax.random.uniform(seeds[5], (QUERIES, B), jnp.float32) ** block_levels(seeds[5], (QUERIES, B), ((0, 32),), -0.2, 0.2), 0.19921875, 1.0).astype(jnp.bfloat16)
    parent_pos = touch_ends(jax.random.randint(seeds[6], (QUERIES, B), 0, B * L), jax.random.fold_in(seeds[6], 1), 0, (B * L) - 1).astype(jnp.int32)
    return dict(queries=queries, weights=weights, block_mask=block_mask, label_map=label_map, beam_lists=beam_lists, root_score=root_score, parent_pos=parent_pos)


def tree_level(queries, scorer, keep_mask, label_map, beam_list, parent):
    groups = scorer.shape[0]
    feature = scorer.shape[1]
    label_width = scorer.shape[2]
    beam_len = beam_list.shape[1]
    flat_beam = beam_list.reshape(-1)
    flat_parent = parent.reshape(-1).astype(jnp.float32)
    most_rows = (QUERIES // QBLK) * CAP

    def visit_group(summed, group_id):
        hitting = flat_beam == group_id
        entries = jnp.nonzero(hitting, size=most_rows, fill_value=0)[0].astype(jnp.int32)
        active = jnp.arange(most_rows, dtype=jnp.int32) < jnp.sum(hitting.astype(jnp.int32))
        routed = queries[entries // beam_len]
        keeping = jnp.repeat(keep_mask[group_id], feature // keep_mask.shape[1]).astype(scorer.dtype)
        masked = scorer[group_id] * keeping[:, None]
        logits = jnp.dot(routed, masked, preferred_element_type=jnp.float32)
        scored = jax.nn.sigmoid(logits) * flat_parent[entries][:, None]
        scored = scored[:, label_map[group_id]]
        scored = jnp.where(active[:, None], scored, jnp.zeros_like(scored))
        return summed.at[entries].add(scored), None

    initial = jnp.zeros((flat_beam.shape[0], label_width), jnp.float32)
    summed, _ = lax.scan(visit_group, initial, jnp.arange(groups, dtype=jnp.int32))
    return summed.reshape(beam_list.shape[0], beam_len, label_width)


def reference(queries, weights, block_mask, label_map, beam_lists, root_score, parent_pos):
    first_level = jnp.zeros((QUERIES, B, L), jnp.float32)
    for member in range(TREES):
        first_level = first_level + tree_level(queries, weights[0, member], block_mask[0, member], label_map[0, member], beam_lists[0], root_score)
    picked = jnp.take_along_axis(first_level.reshape(QUERIES, B * L), parent_pos, axis=1) / TREES
    second_parent = picked.astype(jnp.bfloat16)
    second = jnp.zeros((QUERIES, B, L), jnp.float32)
    for member in range(TREES):
        second = second + tree_level(queries, weights[1, member], block_mask[1, member], label_map[1, member], beam_lists[1], second_parent)
    return jnp.stack([first_level, second])
```

```python
import functools

import jax
import jax.numpy as jnp
from jax import lax
from jax.experimental import pallas as pl
from jax.experimental.pallas import tpu as pltpu
from jax.sharding import PartitionSpec as P

QBLK = 32
CAP = 8
ROWS_OF_CHIPS = 4
MESH = pl.DeviceIdType.MESH
F32, BF16, I32 = jnp.float32, jnp.bfloat16, jnp.int32


def exact_parts(value):
    high = value.astype(BF16)
    rest = value - high.astype(F32)
    middle = rest.astype(BF16)
    return high, middle, (rest - middle.astype(F32)).astype(BF16)


def wait_for(ref, sem):
    pltpu.make_async_copy(ref, ref, sem).wait()


def kernel(
    groups,
    leaves,
    cap,
    q_ref,
    w_ref,
    mask_ref,
    map_ref,
    beam_ref,
    root_ref,
    pos_ref,
    out_ref,
    w_in,
    w_own,
    perm,
    picked,
    rows_in,
    scored,
    half_left,
    half_right,
    block_left,
    block_right,
    total,
    returned,
    choose,
    columns,
    line,
    parent_out,
    parent_in,
    w_sem,
    yz_send,
    yz_recv,
    fwd_send,
    fwd_recv,
    rel_send,
    rel_recv,
    half_send,
    half_recv,
    block_send,
    block_recv,
    ret_send,
    ret_recv,
    parent_send,
    parent_recv,
):
    level = lax.axis_index("level")
    g = lax.axis_index("group")
    x = lax.axis_index("leaf")
    ny = ROWS_OF_CHIPS
    nz = groups // ny
    y, z = g // nz, g % nz
    right, left, across = (x + 1) % leaves, (x + leaves - 1) % leaves, (x + 2) % leaves
    beam_len, queries = beam_ref.shape
    feature, labels = w_ref.shape
    part = feature // leaves
    share = labels // leaves
    slots = groups * cap
    chunk = nz * cap
    half = chunk // 2

    weight_copy = pltpu.make_async_copy(w_ref, w_in, w_sem)
    weight_copy.start()

    barrier = pltpu.get_barrier_semaphore()

    def greet(o, carry):
        pl.semaphore_signal(
            barrier, inc=1, device_id={"group": (g + o) % groups}, device_id_type=MESH
        )
        return carry

    lax.fori_loop(1, groups, greet, 0)
    for other in (left, right):
        pl.semaphore_signal(barrier, inc=1, device_id={"leaf": other}, device_id_type=MESH)
    for other in range(leaves):
        pl.semaphore_signal(
            barrier,
            inc=1,
            device_id={"level": 1 - level, "leaf": other},
            device_id_type=MESH,
        )

    beam = beam_ref[...]
    group_id = lax.broadcasted_iota(I32, (groups, queries), 0)
    hit = jnp.zeros((groups, queries), F32)
    for b in range(beam_len):
        hit = hit + (beam[b : b + 1, :] == group_id).astype(F32)
    earlier = (
        lax.broadcasted_iota(I32, (queries, queries), 0)
        < lax.broadcasted_iota(I32, (queries, queries), 1)
    ).astype(F32)
    rank = jnp.dot(hit.astype(BF16), earlier.astype(BF16), preferred_element_type=F32)
    place = group_id.astype(F32) * cap + rank
    slot = [
        jnp.sum(jnp.where(beam[b : b + 1, :] == group_id, place, 0.0), axis=0, keepdims=True)
        for b in range(beam_len)
    ]
    slot_id = lax.broadcasted_iota(I32, (slots, queries), 0).astype(F32)
    select = jnp.zeros((slots, queries), F32)
    for b in range(beam_len):
        select = select + (slot[b] == slot_id).astype(F32)
    own_part = q_ref[:, pl.ds(pl.multiple_of(x * part, 128), part)]
    chosen_rows = jnp.dot(select.astype(BF16), own_part, preferred_element_type=F32)
    picked[...] = chosen_rows.astype(BF16).reshape(slots // 8, 8, part)

    pl.semaphore_wait(barrier, groups - 1 + 2 + leaves)

    def slot_rows(group):
        return pl.ds(pl.multiple_of(group * cap, 8), cap)

    def slot_blocks(group):
        return pl.ds(group * (cap // 8), cap // 8)

    def chunk_blocks(step):
        return pl.ds(((y + step) % ny) * (chunk // 8), chunk // 8)

    def chunk_half(step, which):
        return pl.ds(((y + step) % ny) * (chunk // 8) + which * (half // 8), half // 8)

    pltpu.make_async_copy(
        picked.at[slot_blocks(g)], rows_in.at[x, slot_blocks(g)], yz_recv.at[0]
    ).start()

    def send_rows(n, carry):
        step = n // nz
        to = ((y + ny - step) % ny) * nz + (z + n) % nz
        pltpu.make_async_remote_copy(
            src_ref=picked.at[slot_blocks(to)],
            dst_ref=rows_in.at[x, slot_blocks(g)],
            send_sem=yz_send,
            recv_sem=yz_recv.at[step],
            device_id={"group": to},
            device_id_type=MESH,
        ).start()
        return carry

    lax.fori_loop(1, groups, send_rows, 0)

    tile = 256
    mask_rows = feature // mask_ref.shape[0]

    def fill_perm(n, carry):
        at = pl.ds(pl.multiple_of(n * tile, tile), tile)
        column = lax.broadcasted_iota(I32, (tile, labels), 0) + n * tile
        perm[at, :] = (column == map_ref[...]).astype(F32).astype(BF16)
        return carry

    lax.fori_loop(0, labels // tile, fill_perm, 0)
    weight_copy.wait()

    def permute(n, carry):
        row = n // (labels // tile)
        at = pl.ds(pl.multiple_of((n % (labels // tile)) * tile, tile), tile)
        product = jnp.dot(
            w_in[pl.ds(pl.multiple_of(row * tile, tile), tile), :],
            perm[:, at],
            preferred_element_type=F32,
        )
        for m in range(tile // mask_rows):
            keep = mask_ref[row * (tile // mask_rows) + m].astype(F32)
            w_own[pl.ds(pl.multiple_of(row * tile + m * mask_rows, mask_rows), mask_rows), at] = (
                product[m * mask_rows : (m + 1) * mask_rows] * keep
            ).astype(BF16)
        return carry

    lax.fori_loop(0, (feature // tile) * (labels // tile), permute, 0)

    pos = pos_ref[...]
    parent_slot, parent_label = pos // labels, (pos % labels).astype(F32)
    root = root_ref[...].astype(F32)
    line[...] = jnp.zeros_like(line)
    for b in range(beam_len):
        line[b : b + 1, :queries] = slot[b]
        line[2 * beam_len + b : 2 * beam_len + b + 1, :queries] = parent_label[b : b + 1]
        line[3 * beam_len + b : 3 * beam_len + b + 1, :queries] = root[b : b + 1]
        slot_of = jnp.zeros((1, queries), F32)
        root_of = jnp.zeros((1, queries), F32)
        for s in range(beam_len):
            same = parent_slot[b : b + 1] == s
            slot_of = slot_of + jnp.where(same, slot[s], 0.0)
            root_of = root_of + jnp.where(same, root[s : s + 1], 0.0)
        line[beam_len + b : beam_len + b + 1, :queries] = slot_of
        line[4 * beam_len + b : 4 * beam_len + b + 1, :queries] = root_of
    columns[...] = jnp.transpose(line[...])
    across_slots = lax.broadcasted_iota(I32, (queries, slots), 1).astype(F32)
    for b in range(2 * beam_len):
        choose[b * queries : (b + 1) * queries, :] = (
            (columns[:queries, b : b + 1] == across_slots).astype(F32).astype(BF16)
        )

    def to_leaf(src, dst, send, recv, other):
        pltpu.make_async_remote_copy(
            src_ref=src,
            dst_ref=dst,
            send_sem=send,
            recv_sem=recv,
            device_id={"leaf": other},
            device_id_type=MESH,
        ).start()

    def stage(t, carry):
        @pl.when(t < ny)
        def _():
            own = rows_in.at[x, chunk_blocks(t)]
            wait_for(own, yz_recv.at[t])
            to_leaf(own, own, fwd_send, fwd_recv.at[0, t], right)
            to_leaf(own, own, fwd_send, fwd_recv.at[1, t], left)

        @pl.when((t >= 1) & (t < ny + 1))
        def _():
            c = t - 1
            wait_for(rows_in.at[left, chunk_blocks(c)], fwd_recv.at[0, c])
            first = rows_in.at[left, chunk_half(c, 0)]
            to_leaf(first, first, rel_send, rel_recv.at[0, c], right)
            wait_for(rows_in.at[right, chunk_blocks(c)], fwd_recv.at[1, c])
            second = rows_in.at[right, chunk_half(c, 1)]
            to_leaf(second, second, rel_send, rel_recv.at[1, c], left)

        @pl.when((t >= 2) & (t < ny + 2))
        def _():
            c = t - 2
            wait_for(rows_in.at[across, chunk_half(c, 0)], rel_recv.at[0, c])
            wait_for(rows_in.at[across, chunk_half(c, 1)], rel_recv.at[1, c])

            def score(n, carry):
                j = (across + n) % leaves
                at = pl.ds(pl.multiple_of(j * share, 128), share)
                logits = jnp.zeros((chunk, share), F32)
                for p in range(leaves):
                    logits = logits + jnp.dot(
                        rows_in[p, chunk_blocks(c)].reshape(chunk, part),
                        w_own[p * part : (p + 1) * part, at],
                        preferred_element_type=F32,
                    )
                scored[c, j] = jax.nn.sigmoid(logits)
                return carry

            lax.fori_loop(0, leaves, score, 0)
            to_leaf(
                scored.at[c, across, pl.ds(0, half)],
                half_left.at[c],
                half_send,
                half_recv.at[0, c],
                right,
            )
            to_leaf(
                scored.at[c, across, pl.ds(half, half)],
                half_right.at[c],
                half_send,
                half_recv.at[1, c],
                left,
            )

        @pl.when((t >= 3) & (t < ny + 3))
        def _():
            c = t - 3
            wait_for(half_left.at[c], half_recv.at[0, c])
            scored[c, right, :half] = scored[c, right, :half] + half_left[c]
            to_leaf(
                scored.at[c, right], block_left.at[c], block_send, block_recv.at[0, c], right
            )
            wait_for(half_right.at[c], half_recv.at[1, c])
            scored[c, left, half:] = scored[c, left, half:] + half_right[c]
            to_leaf(
                scored.at[c, left], block_right.at[c], block_send, block_recv.at[1, c], left
            )

        @pl.when(t >= 4)
        def _():
            c = t - 4
            wait_for(block_left.at[c], block_recv.at[0, c])
            wait_for(block_right.at[c], block_recv.at[1, c])
            total[c] = scored[c, x] + (block_left[c] + block_right[c])
            row = ((y + c) % ny) * nz

            def send_back(n, carry):
                zz = (z + n) % nz
                pltpu.make_async_remote_copy(
                    src_ref=total.at[c, slot_rows(zz)],
                    dst_ref=returned.at[slot_rows(g)],
                    send_sem=ret_send,
                    recv_sem=ret_recv,
                    device_id={"group": row + zz},
                    device_id_type=MESH,
                ).start()
                return carry

            @pl.when(c == 0)
            def _():
                pltpu.make_async_copy(
                    total.at[c, slot_rows(z)], returned.at[slot_rows(g)], ret_recv
                ).start()

            @pl.when(c > 0)
            def _():
                send_back(0, 0)

            lax.fori_loop(1, nz, send_back, 0)

        return carry

    lax.fori_loop(0, ny + 4, stage, 0)

    wait_for(returned, ret_recv)
    high, middle, low = exact_parts(returned[...])
    entries = beam_len * queries

    def gather(at):
        chosen = choose[at, :]
        return (
            jnp.dot(chosen, high, preferred_element_type=F32)
            + jnp.dot(chosen, middle, preferred_element_type=F32)
        ) + jnp.dot(chosen, low, preferred_element_type=F32)

    def to_level_one(other, carry):
        pltpu.make_async_remote_copy(
            src_ref=parent_out,
            dst_ref=parent_in.at[x],
            send_sem=parent_send,
            recv_sem=parent_recv,
            device_id={"level": 1, "leaf": other},
            device_id_type=MESH,
        ).start()
        return carry

    @pl.when(level == 0)
    def _():
        lane = lax.broadcasted_iota(I32, (queries, share), 1).astype(F32) + (x * share).astype(F32)
        wide = lax.broadcasted_iota(I32, (queries, 128), 1)
        sums = gather(slice(entries, 2 * entries))
        parents = jnp.zeros((queries, 128), F32)
        for b in range(beam_len):
            at_label = columns[:queries, 2 * beam_len + b : 2 * beam_len + b + 1] == lane
            mine = jnp.where(at_label, sums[b * queries : (b + 1) * queries], 0.0)
            value = jnp.sum(mine, axis=1, keepdims=True) * columns[
                :queries, 4 * beam_len + b : 4 * beam_len + b + 1
            ]
            parents = jnp.where(wide == b, value, parents)
        parent_out[...] = parents
        lax.fori_loop(0, leaves, to_level_one, 0)

    sums = gather(slice(0, entries))

    @pl.when(level == 0)
    def _():
        for b in range(beam_len):
            out_ref[b] = (
                sums[b * queries : (b + 1) * queries]
                * columns[:queries, 3 * beam_len + b : 3 * beam_len + b + 1]
            )

        wait_for(parent_in, parent_send)

    @pl.when(level == 1)
    def _():
        wait_for(parent_in, parent_recv)
        parents = parent_in[0]
        for n in range(1, leaves):
            parents = parents + parent_in[n]
        parents = (parents / leaves).astype(BF16).astype(F32)
        for b in range(beam_len):
            out_ref[b] = sums[b * queries : (b + 1) * queries] * parents[:, b : b + 1]

    wait_for(picked.at[pl.ds(0, (groups - 1) * cap // 8)], yz_send)
    wait_for(rows_in.at[pl.ds(0, 2)], fwd_send)
    wait_for(rows_in.at[0], rel_send)
    wait_for(total, half_send)
    wait_for(scored.at[:, pl.ds(0, 2)], block_send)
    wait_for(returned.at[pl.ds(0, (groups - 1) * cap)], ret_send)


def body(queries, weights, block_mask, label_map, beam_lists, root_score, parent_pos):
    groups, leaves = lax.axis_size("group"), lax.axis_size("leaf")
    rows, feature = queries.shape
    labels = weights.shape[4]
    beam_len = beam_lists.shape[2]
    cap = rows // QBLK * CAP
    slots = groups * cap
    ny = ROWS_OF_CHIPS
    chunk = slots // ny
    half = chunk // 2
    share = labels // leaves
    vmem = pl.BlockSpec(memory_space=pltpu.VMEM)
    dma = pltpu.SemaphoreType.DMA
    out = pl.pallas_call(
        functools.partial(kernel, groups, leaves, cap),
        out_shape=jax.ShapeDtypeStruct((beam_len, rows, share), F32),
        in_specs=[
            vmem,
            pl.BlockSpec(memory_space=pl.ANY),
            pl.BlockSpec(memory_space=pltpu.SMEM),
            vmem,
            vmem,
            vmem,
            vmem,
        ],
        out_specs=vmem,
        scratch_shapes=[
            pltpu.VMEM((feature, labels), BF16),
            pltpu.VMEM((feature, labels), BF16),
            pltpu.VMEM((labels, labels), BF16),
            pltpu.VMEM((slots // 8, 8, feature // leaves), BF16),
            pltpu.VMEM((leaves, slots // 8, 8, feature // leaves), BF16),
            pltpu.VMEM((ny, leaves, chunk, share), F32),
            pltpu.VMEM((ny, half, share), F32),
            pltpu.VMEM((ny, half, share), F32),
            pltpu.VMEM((ny, chunk, share), F32),
            pltpu.VMEM((ny, chunk, share), F32),
            pltpu.VMEM((ny, chunk, share), F32),
            pltpu.VMEM((slots, share), F32),
            pltpu.VMEM((2 * beam_len * rows, slots), BF16),
            pltpu.VMEM((128, 128), F32),
            pltpu.VMEM((128, 128), F32),
            pltpu.VMEM((rows, 128), F32),
            pltpu.VMEM((leaves, rows, 128), F32),
            dma,
            dma,
            dma((ny,)),
            dma,
            dma((2, ny)),
            dma,
            dma((2, ny)),
            dma,
            dma((2, ny)),
            dma,
            dma((2, ny)),
            dma,
            dma,
            dma,
            dma,
        ],
        compiler_params=pltpu.CompilerParams(
            collective_id=0, has_side_effects=True, vmem_limit_bytes=48 << 20
        ),
    )(
        queries,
        weights[0, 0, 0],
        block_mask[0, 0, 0],
        label_map[0, 0],
        beam_lists[0].T,
        root_score.T,
        parent_pos.T,
    )
    return jnp.transpose(out, (1, 0, 2))[None]


def solution(mesh):
    in_specs = (
        P("group", None),
        P("level", "leaf", "group", None, None),
        P("level", "leaf", "group", None),
        P("level", "leaf", "group", None),
        P("level", "group", None),
        P("group", None),
        P("group", None),
    )
    out_specs = P("level", "group", None, "leaf")
    return jax.shard_map(body, mesh=mesh, in_specs=in_specs, out_specs=out_specs, check_vma=False)
```

```python
import functools

import jax
import jax.numpy as jnp
from jax import lax
from jax.experimental import pallas as pl
from jax.experimental.pallas import tpu as pltpu
from jax.sharding import PartitionSpec as P

QBLK = 32
CAP = 8
ROWS_OF_CHIPS = 4
MESH = pl.DeviceIdType.MESH
F32, BF16, I32, I16 = jnp.float32, jnp.bfloat16, jnp.int32, jnp.int16


def encode(value):
    octaves = jnp.log2(jnp.maximum(value, 2.0**-61))
    return jnp.round((octaves + 29.0) * 1024.0).astype(I32).astype(I16)


def decode(code):
    return jnp.exp2(code.astype(I32).astype(F32) * (1.0 / 1024.0) - 29.0)


def two_parts(value):
    high = value.astype(BF16)
    return high, (value - high.astype(F32)).astype(BF16)


def wait_for(ref, sem):
    pltpu.make_async_copy(ref, ref, sem).wait()


def kernel(
    groups,
    leaves,
    cap,
    q_hbm,
    w_ref,
    mask_hbm,
    map_hbm,
    beam_hbm,
    root_hbm,
    pos_hbm,
    out_ref,
    q_ref,
    mask_ref,
    map_ref,
    beam_ref,
    root_ref,
    pos_ref,
    w_in,
    w_own,
    perm,
    picked,
    rows_in,
    scored,
    half_out,
    block_out,
    half_left,
    half_right,
    block_left,
    block_right,
    total,
    returned,
    choose,
    columns,
    line,
    parent_out,
    parent_in,
    in_sem,
    w_sem,
    yz_send,
    yz_recv,
    fwd_send,
    fwd_recv,
    rel_send,
    rel_recv,
    half_send,
    half_recv,
    block_send,
    block_recv,
    ret_send,
    ret_recv,
    parent_send,
    parent_recv,
):
    level = lax.axis_index("level")
    g = lax.axis_index("group")
    x = lax.axis_index("leaf")
    ny = ROWS_OF_CHIPS
    nz = groups // ny
    y, z = g // nz, g % nz
    right, left, across = (x + 1) % leaves, (x + leaves - 1) % leaves, (x + 2) % leaves
    beam_len, queries = beam_ref.shape
    feature, labels = w_ref.shape
    part = feature // leaves
    share = labels // leaves
    slots = groups * cap
    chunk = nz * cap
    half = chunk // 2

    copies = [
        pltpu.make_async_copy(src, dst, in_sem.at[n])
        for n, (src, dst) in enumerate(
            (
                (beam_hbm, beam_ref),
                (q_hbm, q_ref),
                (map_hbm, map_ref),
                (mask_hbm, mask_ref),
                (pos_hbm, pos_ref),
                (root_hbm, root_ref),
            )
        )
    ]
    for copy in copies:
        copy.start()
    weight_copy = pltpu.make_async_copy(w_ref, w_in, w_sem)
    weight_copy.start()

    barrier = pltpu.get_barrier_semaphore()

    def greet(o, carry):
        pl.semaphore_signal(
            barrier, inc=1, device_id={"group": (g + o) % groups}, device_id_type=MESH
        )
        return carry

    lax.fori_loop(1, groups, greet, 0)
    for other in (left, right):
        pl.semaphore_signal(barrier, inc=1, device_id={"leaf": other}, device_id_type=MESH)
    for other in range(leaves):
        pl.semaphore_signal(
            barrier,
            inc=1,
            device_id={"level": 1 - level, "leaf": other},
            device_id_type=MESH,
        )

    for copy in copies[:2]:
        copy.wait()
    beam = beam_ref[...]
    group_id = lax.broadcasted_iota(I32, (groups, queries), 0)
    hit = jnp.zeros((groups, queries), F32)
    for b in range(beam_len):
        hit = hit + (beam[b : b + 1, :] == group_id).astype(F32)
    earlier = (
        lax.broadcasted_iota(I32, (queries, queries), 0)
        < lax.broadcasted_iota(I32, (queries, queries), 1)
    ).astype(F32)
    rank = jnp.dot(hit.astype(BF16), earlier.astype(BF16), preferred_element_type=F32)
    place = group_id.astype(F32) * cap + rank
    slot = [
        jnp.sum(jnp.where(beam[b : b + 1, :] == group_id, place, 0.0), axis=0, keepdims=True)
        for b in range(beam_len)
    ]
    slot_id = lax.broadcasted_iota(I32, (slots, queries), 0).astype(F32)
    select = jnp.zeros((slots, queries), F32)
    for b in range(beam_len):
        select = select + (slot[b] == slot_id).astype(F32)
    own_part = q_ref[:, pl.ds(pl.multiple_of(x * part, 128), part)]
    chosen_rows = jnp.dot(select.astype(BF16), own_part, preferred_element_type=F32)
    picked[...] = chosen_rows.astype(BF16).reshape(slots // 8, 8, part)

    pl.semaphore_wait(barrier, groups - 1 + 2 + leaves)

    def slot_blocks(group):
        return pl.ds(group * (cap // 8), cap // 8)

    def chunk_blocks(step):
        return pl.ds(((y + step) % ny) * (chunk // 8), chunk // 8)

    def chunk_half(step, which):
        return pl.ds(((y + step) % ny) * (chunk // 8) + which * (half // 8), half // 8)

    pltpu.make_async_copy(
        picked.at[slot_blocks(g)], rows_in.at[x, slot_blocks(g)], yz_recv.at[0]
    ).start()

    def send_rows(n, carry):
        step = n // nz
        to = ((y + ny - step) % ny) * nz + (z + n) % nz
        pltpu.make_async_remote_copy(
            src_ref=picked.at[slot_blocks(to)],
            dst_ref=rows_in.at[x, slot_blocks(g)],
            send_sem=yz_send,
            recv_sem=yz_recv.at[step],
            device_id={"group": to},
            device_id_type=MESH,
        ).start()
        return carry

    lax.fori_loop(1, groups, send_rows, 0)

    for copy in copies[2:]:
        copy.wait()
    tile = 256
    mask_rows = feature // mask_ref.shape[0]

    def fill_perm(n, carry):
        at = pl.ds(pl.multiple_of(n * tile, tile), tile)
        column = lax.broadcasted_iota(I32, (tile, labels), 0) + n * tile
        perm[at, :] = (column == map_ref[...]).astype(F32).astype(BF16)
        return carry

    lax.fori_loop(0, labels // tile, fill_perm, 0)
    weight_copy.wait()

    def permute(n, carry):
        row = n // (labels // tile)
        at = pl.ds(pl.multiple_of((n % (labels // tile)) * tile, tile), tile)
        product = jnp.dot(
            w_in[pl.ds(pl.multiple_of(row * tile, tile), tile), :],
            perm[:, at],
            preferred_element_type=F32,
        )
        for m in range(tile // mask_rows):
            keep = mask_ref[row * (tile // mask_rows) + m].astype(F32)
            w_own[pl.ds(pl.multiple_of(row * tile + m * mask_rows, mask_rows), mask_rows), at] = (
                product[m * mask_rows : (m + 1) * mask_rows] * keep
            ).astype(BF16)
        return carry

    lax.fori_loop(0, (feature // tile) * (labels // tile), permute, 0)

    pos = pos_ref[...]
    parent_slot, parent_label = pos // labels, (pos % labels).astype(F32)
    root = root_ref[...].astype(F32)
    line[...] = jnp.zeros_like(line)
    for b in range(beam_len):
        line[b : b + 1, :queries] = slot[b]
        line[2 * beam_len + b : 2 * beam_len + b + 1, :queries] = parent_label[b : b + 1]
        line[3 * beam_len + b : 3 * beam_len + b + 1, :queries] = root[b : b + 1]
        slot_of = jnp.zeros((1, queries), F32)
        root_of = jnp.zeros((1, queries), F32)
        for s in range(beam_len):
            same = parent_slot[b : b + 1] == s
            slot_of = slot_of + jnp.where(same, slot[s], 0.0)
            root_of = root_of + jnp.where(same, root[s : s + 1], 0.0)
        line[beam_len + b : beam_len + b + 1, :queries] = slot_of
        line[4 * beam_len + b : 4 * beam_len + b + 1, :queries] = root_of
    columns[...] = jnp.transpose(line[...])
    across_slots = lax.broadcasted_iota(I32, (queries, slots), 1).astype(F32)
    for b in range(2 * beam_len):
        choose[b * queries : (b + 1) * queries, :] = (
            (columns[:queries, b : b + 1] == across_slots).astype(F32).astype(BF16)
        )

    def to_leaf(src, dst, send, recv, other):
        pltpu.make_async_remote_copy(
            src_ref=src,
            dst_ref=dst,
            send_sem=send,
            recv_sem=recv,
            device_id={"leaf": other},
            device_id_type=MESH,
        ).start()

    def stage(t, carry):
        @pl.when(t < ny)
        def _():
            own = rows_in.at[x, chunk_blocks(t)]
            wait_for(own, yz_recv.at[t])
            to_leaf(own, own, fwd_send, fwd_recv.at[0, t], right)
            to_leaf(own, own, fwd_send, fwd_recv.at[1, t], left)

        @pl.when((t >= 1) & (t < ny + 1))
        def _():
            c = t - 1
            wait_for(rows_in.at[left, chunk_blocks(c)], fwd_recv.at[0, c])
            first = rows_in.at[left, chunk_half(c, 0)]
            to_leaf(first, first, rel_send, rel_recv.at[0, c], right)
            wait_for(rows_in.at[right, chunk_blocks(c)], fwd_recv.at[1, c])
            second = rows_in.at[right, chunk_half(c, 1)]
            to_leaf(second, second, rel_send, rel_recv.at[1, c], left)

        @pl.when((t >= 2) & (t < ny + 2))
        def _():
            c = t - 2
            wait_for(rows_in.at[across, chunk_half(c, 0)], rel_recv.at[0, c])
            wait_for(rows_in.at[across, chunk_half(c, 1)], rel_recv.at[1, c])

            def score(n, carry):
                j = (across + n) % leaves
                at = pl.ds(pl.multiple_of(j * share, 128), share)
                logits = jnp.zeros((chunk, share), F32)
                for p in range(leaves):
                    logits = logits + jnp.dot(
                        rows_in[p, chunk_blocks(c)].reshape(chunk, part),
                        w_own[p * part : (p + 1) * part, at],
                        preferred_element_type=F32,
                    )
                scored[c, j] = jax.nn.sigmoid(logits)
                return carry

            lax.fori_loop(0, leaves, score, 0)
            half_out[c] = encode(scored[c, across])
            to_leaf(
                half_out.at[c, pl.ds(0, half)],
                half_left.at[c],
                half_send,
                half_recv.at[0, c],
                right,
            )
            to_leaf(
                half_out.at[c, pl.ds(half, half)],
                half_right.at[c],
                half_send,
                half_recv.at[1, c],
                left,
            )

        @pl.when((t >= 3) & (t < ny + 3))
        def _():
            c = t - 3
            wait_for(half_left.at[c], half_recv.at[0, c])
            block_out[c, 0, :half] = encode(scored[c, right, :half] + decode(half_left[c]))
            block_out[c, 0, half:] = encode(scored[c, right, half:])
            to_leaf(
                block_out.at[c, 0], block_left.at[c], block_send, block_recv.at[0, c], right
            )
            wait_for(half_right.at[c], half_recv.at[1, c])
            block_out[c, 1, :half] = encode(scored[c, left, :half])
            block_out[c, 1, half:] = encode(scored[c, left, half:] + decode(half_right[c]))
            to_leaf(
                block_out.at[c, 1], block_right.at[c], block_send, block_recv.at[1, c], left
            )

        @pl.when(t >= 4)
        def _():
            c = t - 4
            wait_for(block_left.at[c], block_recv.at[0, c])
            wait_for(block_right.at[c], block_recv.at[1, c])
            sums = scored[c, x] + (decode(block_left[c]) + decode(block_right[c]))
            total[c] = encode(sums.reshape(chunk // 8, 8, share))
            row = ((y + c) % ny) * nz

            def send_back(n, carry):
                zz = (z + n) % nz
                pltpu.make_async_remote_copy(
                    src_ref=total.at[c, slot_blocks(zz)],
                    dst_ref=returned.at[slot_blocks(g)],
                    send_sem=ret_send,
                    recv_sem=ret_recv,
                    device_id={"group": row + zz},
                    device_id_type=MESH,
                ).start()
                return carry

            @pl.when(c == 0)
            def _():
                pltpu.make_async_copy(
                    total.at[c, slot_blocks(z)], returned.at[slot_blocks(g)], ret_recv
                ).start()

            @pl.when(c > 0)
            def _():
                send_back(0, 0)

            lax.fori_loop(1, nz, send_back, 0)

        return carry

    lax.fori_loop(0, ny + 4, stage, 0)

    wait_for(returned, ret_recv)
    high, low = two_parts(decode(returned[...]).reshape(slots, share))
    entries = beam_len * queries

    def gather(at):
        chosen = choose[at, :]
        return jnp.dot(chosen, high, preferred_element_type=F32) + jnp.dot(
            chosen, low, preferred_element_type=F32
        )

    def to_level_one(other, carry):
        pltpu.make_async_remote_copy(
            src_ref=parent_out,
            dst_ref=parent_in.at[x],
            send_sem=parent_send,
            recv_sem=parent_recv,
            device_id={"level": 1, "leaf": other},
            device_id_type=MESH,
        ).start()
        return carry

    @pl.when(level == 0)
    def _():
        lane = lax.broadcasted_iota(I32, (queries, share), 1).astype(F32) + (x * share).astype(F32)
        wide = lax.broadcasted_iota(I32, (queries, 128), 1)
        sums = gather(slice(entries, 2 * entries))
        parents = jnp.zeros((queries, 128), F32)
        for b in range(beam_len):
            at_label = columns[:queries, 2 * beam_len + b : 2 * beam_len + b + 1] == lane
            mine = jnp.where(at_label, sums[b * queries : (b + 1) * queries], 0.0)
            value = jnp.sum(mine, axis=1, keepdims=True) * columns[
                :queries, 4 * beam_len + b : 4 * beam_len + b + 1
            ]
            parents = jnp.where(wide == b, value, parents)
        parent_out[...] = parents
        lax.fori_loop(0, leaves, to_level_one, 0)

    sums = gather(slice(0, entries))

    @pl.when(level == 0)
    def _():
        for b in range(beam_len):
            out_ref[b] = (
                sums[b * queries : (b + 1) * queries]
                * columns[:queries, 3 * beam_len + b : 3 * beam_len + b + 1]
            )

        wait_for(parent_in, parent_send)

    @pl.when(level == 1)
    def _():
        wait_for(parent_in, parent_recv)
        parents = parent_in[0]
        for n in range(1, leaves):
            parents = parents + parent_in[n]
        parents = (parents / leaves).astype(BF16).astype(F32)
        for b in range(beam_len):
            out_ref[b] = sums[b * queries : (b + 1) * queries] * parents[:, b : b + 1]

    wait_for(picked.at[pl.ds(0, (groups - 1) * cap // 8)], yz_send)
    wait_for(rows_in.at[pl.ds(0, 2)], fwd_send)
    wait_for(rows_in.at[0], rel_send)
    wait_for(half_out, half_send)
    wait_for(block_out, block_send)
    wait_for(returned.at[pl.ds(0, (groups - 1) * cap // 8)], ret_send)


def body(queries, weights, block_mask, label_map, beam_lists, root_score, parent_pos):
    groups, leaves = lax.axis_size("group"), lax.axis_size("leaf")
    rows, feature = queries.shape
    labels = weights.shape[4]
    beam_len = beam_lists.shape[2]
    cap = rows // QBLK * CAP
    slots = groups * cap
    ny = ROWS_OF_CHIPS
    chunk = slots // ny
    half = chunk // 2
    share = labels // leaves
    vmem = pl.BlockSpec(memory_space=pltpu.VMEM)
    dma = pltpu.SemaphoreType.DMA
    out = pl.pallas_call(
        functools.partial(kernel, groups, leaves, cap),
        out_shape=jax.ShapeDtypeStruct((beam_len, rows, share), F32),
        in_specs=[pl.BlockSpec(memory_space=pltpu.HBM)] * 7,
        out_specs=vmem,
        scratch_shapes=[
            pltpu.VMEM((rows, feature), BF16),
            pltpu.SMEM((block_mask.shape[3],), I32),
            pltpu.VMEM((1, labels), I32),
            pltpu.VMEM((beam_len, rows), I32),
            pltpu.VMEM((beam_len, rows), BF16),
            pltpu.VMEM((beam_len, rows), I32),
            pltpu.VMEM((feature, labels), BF16),
            pltpu.VMEM((feature, labels), BF16),
            pltpu.VMEM((labels, labels), BF16),
            pltpu.VMEM((slots // 8, 8, feature // leaves), BF16),
            pltpu.VMEM((leaves, slots // 8, 8, feature // leaves), BF16),
            pltpu.VMEM((ny, leaves, chunk, share), F32),
            pltpu.VMEM((ny, chunk, share), I16),
            pltpu.VMEM((ny, 2, chunk, share), I16),
            pltpu.VMEM((ny, half, share), I16),
            pltpu.VMEM((ny, half, share), I16),
            pltpu.VMEM((ny, chunk, share), I16),
            pltpu.VMEM((ny, chunk, share), I16),
            pltpu.VMEM((ny, chunk // 8, 8, share), I16),
            pltpu.VMEM((slots // 8, 8, share), I16),
            pltpu.VMEM((2 * beam_len * rows, slots), BF16),
            pltpu.VMEM((128, 128), F32),
            pltpu.VMEM((128, 128), F32),
            pltpu.VMEM((rows, 128), F32),
            pltpu.VMEM((leaves, rows, 128), F32),
            dma((6,)),
            dma,
            dma,
            dma((ny,)),
            dma,
            dma((2, ny)),
            dma,
            dma((2, ny)),
            dma,
            dma((2, ny)),
            dma,
            dma((2, ny)),
            dma,
            dma,
            dma,
            dma,
        ],
        compiler_params=pltpu.CompilerParams(
            collective_id=0, has_side_effects=True, vmem_limit_bytes=60 << 20
        ),
    )(
        queries,
        weights[0, 0, 0],
        block_mask[0, 0, 0],
        label_map[0, 0],
        beam_lists[0].T,
        root_score.T,
        parent_pos.T,
    )
    return jnp.transpose(out, (1, 0, 2))[None]


def solution(mesh):
    in_specs = (
        P("group", None),
        P("level", "leaf", "group", None, None),
        P("level", "leaf", "group", None),
        P("level", "leaf", "group", None),
        P("level", "group", None),
        P("group", None),
        P("group", None),
    )
    out_specs = P("level", "group", None, "leaf")
    return jax.shard_map(body, mesh=mesh, in_specs=in_specs, out_specs=out_specs, check_vma=False)
```

```python
import functools

import jax
import jax.numpy as jnp
from jax import lax
from jax.experimental import pallas as pl
from jax.experimental.pallas import tpu as pltpu
from jax.sharding import PartitionSpec as P

QBLK = 32
CAP = 8
ROWS_OF_CHIPS = 4
MESH = pl.DeviceIdType.MESH
F32, BF16, I32, I16 = jnp.float32, jnp.bfloat16, jnp.int32, jnp.int16


def encode(value):
    octaves = jnp.log2(jnp.maximum(value, 2.0**-61))
    return jnp.round((octaves + 29.0) * 1024.0).astype(I32).astype(I16)


def decode(code):
    return jnp.exp2(code.astype(I32).astype(F32) * (1.0 / 1024.0) - 29.0)


def two_parts(value):
    high = value.astype(BF16)
    return high, (value - high.astype(F32)).astype(BF16)


def wait_for(ref, sem):
    pltpu.make_async_copy(ref, ref, sem).wait()


def kernel(
    groups,
    leaves,
    cap,
    q_hbm,
    w_ref,
    mask_hbm,
    map_hbm,
    beam_hbm,
    root_hbm,
    pos_hbm,
    out_ref,
    q_ref,
    mask_ref,
    map_ref,
    beam_ref,
    root_ref,
    pos_ref,
    w_in,
    w_own,
    perm,
    spread,
    beams_own,
    beams_in,
    hits,
    select,
    picked,
    rows_in,
    scored,
    half_out,
    block_out,
    half_left,
    half_right,
    block_left,
    block_right,
    total,
    returned,
    choose,
    columns,
    line,
    parent_out,
    parent_in,
    in_sem,
    w_sem,
    beam_send,
    beam_recv,
    z_send,
    z_recv,
    y_send,
    y_recv,
    fwd_send,
    fwd_recv,
    half_send,
    half_recv,
    block_send,
    block_recv,
    ret_send,
    ret_recv,
    parent_send,
    parent_recv,
):
    level = lax.axis_index("level")
    g = lax.axis_index("group")
    x = lax.axis_index("leaf")
    ny = ROWS_OF_CHIPS
    nz = groups // ny
    y, z = g // nz, g % nz
    right, left, across = (x + 1) % leaves, (x + leaves - 1) % leaves, (x + 2) % leaves
    fetched = 2 * (x % 2)
    other_two = 2 - fetched
    own_part = fetched + level
    beam_len, queries = beam_ref.shape
    feature, labels = w_ref.shape
    part = feature // leaves
    share = labels // leaves
    slots = groups * cap
    chunk = nz * cap
    half = chunk // 2

    copies = [
        pltpu.make_async_copy(src, dst, in_sem.at[n])
        for n, (src, dst) in enumerate(
            (
                (beam_hbm, beam_ref),
                (q_hbm, q_ref),
                (map_hbm, map_ref),
                (mask_hbm, mask_ref),
                (pos_hbm, pos_ref),
                (root_hbm, root_ref),
            )
        )
    ]
    for copy in copies:
        copy.start()
    weight_copy = pltpu.make_async_copy(w_ref, w_in, w_sem)
    weight_copy.start()

    barrier = pltpu.get_barrier_semaphore()

    def greet(o, carry):
        pl.semaphore_signal(
            barrier, inc=1, device_id={"group": (g + o) % groups}, device_id_type=MESH
        )
        return carry

    lax.fori_loop(1, groups, greet, 0)
    for other in (left, right):
        pl.semaphore_signal(barrier, inc=1, device_id={"leaf": other}, device_id_type=MESH)
    for n in range(1, leaves):
        pl.semaphore_signal(
            barrier,
            inc=1,
            device_id={"level": 1 - level, "leaf": (x + n) % leaves},
            device_id_type=MESH,
        )
    for n in range(nz):
        pl.semaphore_signal(
            barrier,
            inc=1,
            device_id={"level": 1 - level, "group": y * nz + (z + n) % nz},
            device_id_type=MESH,
        )
    for n in range(1, ny):
        pl.semaphore_signal(
            barrier,
            inc=1,
            device_id={"level": 1 - level, "group": ((y + n) % ny) * nz + z},
            device_id_type=MESH,
        )

    for copy in copies[:2]:
        copy.wait()
    beam = beam_ref[...]
    group_id = lax.broadcasted_iota(I32, (groups, queries), 0)
    hit = jnp.zeros((groups, queries), F32)
    for b in range(beam_len):
        hit = hit + (beam[b : b + 1, :] == group_id).astype(F32)
    earlier = (
        lax.broadcasted_iota(I32, (queries, queries), 0)
        < lax.broadcasted_iota(I32, (queries, queries), 1)
    ).astype(F32)
    rank = jnp.dot(hit.astype(BF16), earlier.astype(BF16), preferred_element_type=F32)
    place = group_id.astype(F32) * cap + rank
    slot = [
        jnp.sum(jnp.where(beam[b : b + 1, :] == group_id, place, 0.0), axis=0, keepdims=True)
        for b in range(beam_len)
    ]
    spread[0] = q_ref[:, pl.ds(pl.multiple_of(own_part * part, 128), part)]
    beams_own[...] = jnp.full_like(beams_own, -1)
    beams_own[:beam_len, :queries] = beam

    pl.semaphore_wait(barrier, groups - 1 + 2 + leaves - 1 + nz + ny - 1)

    def along_z(src, dst, at, step):
        pltpu.make_async_remote_copy(
            src_ref=src,
            dst_ref=dst,
            send_sem=z_send,
            recv_sem=z_recv.at[at],
            device_id={"group": y * nz + (z + nz + step) % nz},
            device_id_type=MESH,
        ).start()

    pltpu.make_async_copy(beams_own, beams_in.at[level * nz], beam_recv).start()
    for n in range(nz):
        at = 2 * n if n < nz // 2 else 2 * (nz - n) - 1
        for flip in range(2):
            if n or flip:
                pltpu.make_async_remote_copy(
                    src_ref=beams_own,
                    dst_ref=beams_in.at[level * nz + at],
                    send_sem=beam_send,
                    recv_sem=beam_recv,
                    device_id={
                        "level": (level + flip) % 2,
                        "group": y * nz + (z + n) % nz,
                    },
                    device_id_type=MESH,
                ).start()
    along_z(spread.at[0], spread.at[2], 2, 1)
    along_z(spread.at[0], spread.at[1], 1, -1)

    wait_for(beams_in, beam_recv)
    eight = lax.broadcasted_iota(I32, (8, 128), 0)
    near_group = jnp.where(eight < ny, eight * nz + z, -2)

    def find_hits(n, carry):
        names = beams_in[n]
        found = jnp.zeros((8, 128), F32)
        for b in range(beam_len):
            found = found + (names[b : b + 1, :] == near_group).astype(F32)
        hits[pl.ds(pl.multiple_of(n * 8, 8), 8), :] = found
        return carry

    lax.fori_loop(0, 2 * nz, find_hits, 0)
    before = (
        lax.broadcasted_iota(I32, (128, 128), 0) < lax.broadcasted_iota(I32, (128, 128), 1)
    ).astype(F32)
    hits[...] = jnp.dot(
        hits[...].astype(BF16), before.astype(BF16), preferred_element_type=F32
    )
    near_slot = lax.broadcasted_iota(I32, (ny * cap, 128), 0).astype(F32)

    def make_select(n, carry):
        names = beams_in[n]
        place = eight.astype(F32) * cap + hits[pl.ds(pl.multiple_of(n * 8, 8), 8), :] + 1.0
        chosen = jnp.zeros((ny * cap, 128), F32)
        for b in range(beam_len):
            at = jnp.sum(
                jnp.where(names[b : b + 1, :] == near_group, place, 0.0), axis=0, keepdims=True
            )
            chosen = chosen + (at - 1.0 == near_slot).astype(F32)
        select[n % nz, pl.ds(pl.multiple_of((n // nz) * ny * cap, 16), ny * cap), :] = chosen.astype(
            BF16
        )
        return carry

    lax.fori_loop(0, 2 * nz, make_select, 0)

    blocks = cap // 8

    def slot_blocks(group):
        return pl.ds(group * blocks, blocks)

    def chunk_blocks(step):
        return pl.ds(step * (chunk // 8), chunk // 8)

    def distance_blocks(at):
        return pl.ds(at * (half // 8), half // 8)

    def pick(at):
        rows = jnp.dot(select[at, :, :queries], spread[at], preferred_element_type=F32)
        picked[pl.ds(at * (chunk // 8), chunk // 8)] = rows.astype(BF16).reshape(
            chunk // 8, 8, part
        )

        def send_rows(n, carry):
            to_level, to_row = (level + n // ny) % 2, (y + n) % ny
            pltpu.make_async_remote_copy(
                src_ref=picked.at[slot_blocks((at * 2 + to_level) * ny + to_row)],
                dst_ref=rows_in.at[own_part, slot_blocks(at * ny + y)],
                send_sem=y_send,
                recv_sem=y_recv.at[at // 2],
                device_id={"level": to_level, "group": to_row * nz + z},
                device_id_type=MESH,
            ).start()
            return carry

        pltpu.make_async_copy(
            picked.at[slot_blocks((at * 2 + level) * ny + y)],
            rows_in.at[own_part, slot_blocks(at * ny + y)],
            y_recv.at[at // 2],
        ).start()
        lax.fori_loop(1, 2 * ny, send_rows, 0)

    def to_leaf(src, dst, send, recv, other):
        pltpu.make_async_remote_copy(
            src_ref=src,
            dst_ref=dst,
            send_sem=send,
            recv_sem=recv,
            device_id={"leaf": other},
            device_id_type=MESH,
        ).start()

    def exchange(c):
        two = pl.ds(fetched, 2)
        wait_for(rows_in.at[two, chunk_blocks(c)], y_recv.at[c])
        for n, other in enumerate((right, left)):
            rows = rows_in.at[two, distance_blocks(2 * c + n)]
            to_leaf(rows, rows, fwd_send, fwd_recv.at[n, c], other)

    for copy in copies[2:]:
        copy.wait()
    tile = 256
    mask_rows = feature // mask_ref.shape[0]

    def fill_perm(n, carry):
        at = pl.ds(pl.multiple_of(n * tile, tile), tile)
        column = lax.broadcasted_iota(I32, (tile, labels), 0) + n * tile
        perm[at, :] = (column == map_ref[...]).astype(F32).astype(BF16)
        return carry

    lax.fori_loop(0, labels // tile, fill_perm, 0)
    weight_copy.wait()

    def permute(n, carry):
        row = n // (labels // tile)
        at = pl.ds(pl.multiple_of((n % (labels // tile)) * tile, tile), tile)
        product = jnp.dot(
            w_in[pl.ds(pl.multiple_of(row * tile, tile), tile), :],
            perm[:, at],
            preferred_element_type=F32,
        )
        for m in range(tile // mask_rows):
            keep = mask_ref[row * (tile // mask_rows) + m].astype(F32)
            w_own[pl.ds(pl.multiple_of(row * tile + m * mask_rows, mask_rows), mask_rows), at] = (
                product[m * mask_rows : (m + 1) * mask_rows] * keep
            ).astype(BF16)
        return carry

    tiles = (feature // tile) * (labels // tile)
    for c in range(ny):
        up, down = 2 * c, 2 * c + 1
        if c:
            wait_for(spread.at[up], z_recv.at[up])
            if c < ny - 1:
                along_z(spread.at[up], spread.at[up + 2], up + 2, 1)
            else:
                top = pl.ds(0, queries // 2)
                along_z(spread.at[up, top], spread.at[nz - 1, top], nz - 1, 1)
        else:
            pick(0)
        wait_for(spread.at[down], z_recv.at[down])
        if c < ny - 2:
            along_z(spread.at[down], spread.at[down + 2], down + 2, -1)
        elif c == ny - 2:
            low = pl.ds(queries // 2, queries // 2)
            along_z(spread.at[down, low], spread.at[nz - 1, low], nz - 1, -1)
        if c:
            pick(up)
        pick(down)
        if c >= 2:
            exchange(c - 2)
        lax.fori_loop(tiles * c // ny, tiles * (c + 1) // ny, permute, 0)

    pos = pos_ref[...]
    parent_slot, parent_label = pos // labels, (pos % labels).astype(F32)
    root = root_ref[...].astype(F32)
    line[...] = jnp.zeros_like(line)
    for b in range(beam_len):
        line[b : b + 1, :queries] = slot[b]
        line[2 * beam_len + b : 2 * beam_len + b + 1, :queries] = parent_label[b : b + 1]
        line[3 * beam_len + b : 3 * beam_len + b + 1, :queries] = root[b : b + 1]
        slot_of = jnp.zeros((1, queries), F32)
        root_of = jnp.zeros((1, queries), F32)
        for s in range(beam_len):
            same = parent_slot[b : b + 1] == s
            slot_of = slot_of + jnp.where(same, slot[s], 0.0)
            root_of = root_of + jnp.where(same, root[s : s + 1], 0.0)
        line[beam_len + b : beam_len + b + 1, :queries] = slot_of
        line[4 * beam_len + b : 4 * beam_len + b + 1, :queries] = root_of
    columns[...] = jnp.transpose(line[...])
    across_slots = lax.broadcasted_iota(I32, (queries, slots), 1).astype(F32)
    for b in range(2 * beam_len):
        choose[b * queries : (b + 1) * queries, :] = (
            (columns[:queries, b : b + 1] == across_slots).astype(F32).astype(BF16)
        )

    def stage(t, carry):
        @pl.when(t < 2)
        def _():
            exchange(t + ny - 2)

        @pl.when(t < ny)
        def _():
            c = t
            two = pl.ds(other_two, 2)
            for n in range(2):
                wait_for(rows_in.at[two, distance_blocks(2 * c + n)], fwd_recv.at[n, c])

            def score(n, carry):
                j = (across + n) % leaves
                at = pl.ds(pl.multiple_of(j * share, 128), share)
                logits = jnp.zeros((chunk, share), F32)
                for p in range(leaves):
                    logits = logits + jnp.dot(
                        rows_in[p, chunk_blocks(c)].reshape(chunk, part),
                        w_own[p * part : (p + 1) * part, at],
                        preferred_element_type=F32,
                    )
                scored[c, j] = jax.nn.sigmoid(logits)
                return carry

            lax.fori_loop(0, leaves, score, 0)
            half_out[c] = encode(scored[c, across])
            to_leaf(
                half_out.at[c, pl.ds(0, half)],
                half_left.at[c],
                half_send,
                half_recv.at[0, c],
                right,
            )
            to_leaf(
                half_out.at[c, pl.ds(half, half)],
                half_right.at[c],
                half_send,
                half_recv.at[1, c],
                left,
            )

        @pl.when((t >= 1) & (t < ny + 1))
        def _():
            c = t - 1
            wait_for(half_left.at[c], half_recv.at[0, c])
            block_out[c, 0, :half] = encode(scored[c, right, :half] + decode(half_left[c]))
            block_out[c, 0, half:] = encode(scored[c, right, half:])
            to_leaf(
                block_out.at[c, 0], block_left.at[c], block_send, block_recv.at[0, c], right
            )
            wait_for(half_right.at[c], half_recv.at[1, c])
            block_out[c, 1, :half] = encode(scored[c, left, :half])
            block_out[c, 1, half:] = encode(scored[c, left, half:] + decode(half_right[c]))
            to_leaf(
                block_out.at[c, 1], block_right.at[c], block_send, block_recv.at[1, c], left
            )

        @pl.when(t >= 2)
        def _():
            c = t - 2
            wait_for(block_left.at[c], block_recv.at[0, c])
            wait_for(block_right.at[c], block_recv.at[1, c])
            sums = scored[c, x] + (decode(block_left[c]) + decode(block_right[c]))
            total[c] = encode(sums.reshape(chunk // 8, 8, share))

            def send_back(n, carry):
                row = (y + n) % ny
                place = jnp.where(n < ny, z + nz - c, z + c + 1) % nz
                pltpu.make_async_remote_copy(
                    src_ref=total.at[c, slot_blocks((n // ny) * ny + row)],
                    dst_ref=returned.at[slot_blocks(g)],
                    send_sem=ret_send,
                    recv_sem=ret_recv,
                    device_id={"group": row * nz + place},
                    device_id_type=MESH,
                ).start()
                return carry

            @pl.when(c == 0)
            def _():
                pltpu.make_async_copy(
                    total.at[c, slot_blocks(y)], returned.at[slot_blocks(g)], ret_recv
                ).start()

            @pl.when(c > 0)
            def _():
                send_back(0, 0)

            lax.fori_loop(1, 2 * ny, send_back, 0)

        return carry

    lax.fori_loop(0, ny + 2, stage, 0)

    wait_for(returned, ret_recv)
    high, low = two_parts(decode(returned[...]).reshape(slots, share))
    entries = beam_len * queries

    def gather(at):
        chosen = choose[at, :]
        return jnp.dot(chosen, high, preferred_element_type=F32) + jnp.dot(
            chosen, low, preferred_element_type=F32
        )

    def to_level_one(other, carry):
        pltpu.make_async_remote_copy(
            src_ref=parent_out,
            dst_ref=parent_in.at[x],
            send_sem=parent_send,
            recv_sem=parent_recv,
            device_id={"level": 1, "leaf": other},
            device_id_type=MESH,
        ).start()
        return carry

    @pl.when(level == 0)
    def _():
        lane = lax.broadcasted_iota(I32, (queries, share), 1).astype(F32) + (x * share).astype(F32)
        wide = lax.broadcasted_iota(I32, (queries, 128), 1)
        sums = gather(slice(entries, 2 * entries))
        parents = jnp.zeros((queries, 128), F32)
        for b in range(beam_len):
            at_label = columns[:queries, 2 * beam_len + b : 2 * beam_len + b + 1] == lane
            mine = jnp.where(at_label, sums[b * queries : (b + 1) * queries], 0.0)
            value = jnp.sum(mine, axis=1, keepdims=True) * columns[
                :queries, 4 * beam_len + b : 4 * beam_len + b + 1
            ]
            parents = jnp.where(wide == b, value, parents)
        parent_out[...] = parents
        lax.fori_loop(0, leaves, to_level_one, 0)

    sums = gather(slice(0, entries))

    @pl.when(level == 0)
    def _():
        for b in range(beam_len):
            out_ref[b] = (
                sums[b * queries : (b + 1) * queries]
                * columns[:queries, 3 * beam_len + b : 3 * beam_len + b + 1]
            )

        wait_for(parent_in, parent_send)

    @pl.when(level == 1)
    def _():
        wait_for(parent_in, parent_recv)
        parents = parent_in[0]
        for n in range(1, leaves):
            parents = parents + parent_in[n]
        parents = (parents / leaves).astype(BF16).astype(F32)
        for b in range(beam_len):
            out_ref[b] = sums[b * queries : (b + 1) * queries] * parents[:, b : b + 1]

    wait_for(beams_in.at[pl.ds(0, 2 * nz - 1)], beam_send)
    wait_for(spread.at[pl.ds(0, nz - 1)], z_send)
    wait_for(picked.at[pl.ds(0, (2 * groups - nz) * blocks)], y_send)
    wait_for(rows_in.at[pl.ds(0, 2)], fwd_send)
    wait_for(half_out, half_send)
    wait_for(block_out, block_send)
    wait_for(returned.at[pl.ds(0, (groups - 1) * cap // 8)], ret_send)


def body(queries, weights, block_mask, label_map, beam_lists, root_score, parent_pos):
    groups, leaves = lax.axis_size("group"), lax.axis_size("leaf")
    rows, feature = queries.shape
    labels = weights.shape[4]
    beam_len = beam_lists.shape[2]
    cap = rows // QBLK * CAP
    slots = groups * cap
    ny = ROWS_OF_CHIPS
    nz = groups // ny
    chunk = slots // ny
    half = chunk // 2
    share = labels // leaves
    vmem = pl.BlockSpec(memory_space=pltpu.VMEM)
    dma = pltpu.SemaphoreType.DMA
    out = pl.pallas_call(
        functools.partial(kernel, groups, leaves, cap),
        out_shape=jax.ShapeDtypeStruct((beam_len, rows, share), F32),
        in_specs=[pl.BlockSpec(memory_space=pltpu.HBM)] * 7,
        out_specs=vmem,
        scratch_shapes=[
            pltpu.VMEM((rows, feature), BF16),
            pltpu.SMEM((block_mask.shape[3],), I32),
            pltpu.VMEM((1, labels), I32),
            pltpu.VMEM((beam_len, rows), I32),
            pltpu.VMEM((beam_len, rows), BF16),
            pltpu.VMEM((beam_len, rows), I32),
            pltpu.VMEM((feature, labels), BF16),
            pltpu.VMEM((feature, labels), BF16),
            pltpu.VMEM((labels, labels), BF16),
            pltpu.VMEM((nz, rows, feature // leaves), BF16),
            pltpu.VMEM((8, 128), I32),
            pltpu.VMEM((2 * nz, 8, 128), I32),
            pltpu.VMEM((16 * nz, 128), F32),
            pltpu.VMEM((nz, chunk, 128), BF16),
            pltpu.VMEM((2 * slots // 8, 8, feature // leaves), BF16),
            pltpu.VMEM((leaves, slots // 8, 8, feature // leaves), BF16),
            pltpu.VMEM((ny, leaves, chunk, share), F32),
            pltpu.VMEM((ny, chunk, share), I16),
            pltpu.VMEM((ny, 2, chunk, share), I16),
            pltpu.VMEM((ny, half, share), I16),
            pltpu.VMEM((ny, half, share), I16),
            pltpu.VMEM((ny, chunk, share), I16),
            pltpu.VMEM((ny, chunk, share), I16),
            pltpu.VMEM((ny, chunk // 8, 8, share), I16),
            pltpu.VMEM((slots // 8, 8, share), I16),
            pltpu.VMEM((2 * beam_len * rows, slots), BF16),
            pltpu.VMEM((128, 128), F32),
            pltpu.VMEM((128, 128), F32),
            pltpu.VMEM((rows, 128), F32),
            pltpu.VMEM((leaves, rows, 128), F32),
            dma((6,)),
            dma,
            dma,
            dma,
            dma,
            dma((nz,)),
            dma,
            dma((ny,)),
            dma,
            dma((2, ny)),
            dma,
            dma((2, ny)),
            dma,
            dma((2, ny)),
            dma,
            dma,
            dma,
            dma,
        ],
        compiler_params=pltpu.CompilerParams(
            collective_id=0, has_side_effects=True, vmem_limit_bytes=60 << 20
        ),
    )(
        queries,
        weights[0, 0, 0],
        block_mask[0, 0, 0],
        label_map[0, 0],
        beam_lists[0].T,
        root_score.T,
        parent_pos.T,
    )
    return jnp.transpose(out, (1, 0, 2))[None]


def solution(mesh):
    in_specs = (
        P("group", None),
        P("level", "leaf", "group", None, None),
        P("level", "leaf", "group", None),
        P("level", "leaf", "group", None),
        P("level", "group", None),
        P("group", None),
        P("group", None),
    )
    out_specs = P("level", "group", None, "leaf")
    return jax.shard_map(body, mesh=mesh, in_specs=in_specs, out_specs=out_specs, check_vma=False)
```

```python
import functools

import jax
import jax.numpy as jnp
from jax import lax
from jax.experimental import pallas as pl
from jax.experimental.pallas import tpu as pltpu
from jax.sharding import PartitionSpec as P

QBLK = 32
CAP = 8
ROWS_OF_CHIPS = 4
MESH = pl.DeviceIdType.MESH
F32, BF16, I32, I16 = jnp.float32, jnp.bfloat16, jnp.int32, jnp.int16


def encode(value):
    octaves = jnp.log2(jnp.maximum(value, 2.0**-61))
    return jnp.round((octaves + 29.0) * 1024.0).astype(I32).astype(I16)


def decode(code):
    return jnp.exp2(code.astype(I32).astype(F32) * (1.0 / 1024.0) - 29.0)


def two_parts(value):
    high = value.astype(BF16)
    return high, (value - high.astype(F32)).astype(BF16)


def wait_for(ref, sem):
    pltpu.make_async_copy(ref, ref, sem).wait()


def kernel(
    groups,
    leaves,
    cap,
    q_hbm,
    w_ref,
    mask_hbm,
    map_hbm,
    beam_hbm,
    root_hbm,
    pos_hbm,
    out_ref,
    q_ref,
    mask_ref,
    map_ref,
    beam_ref,
    root_ref,
    pos_ref,
    w_in,
    w_own,
    perm,
    spread,
    beams_own,
    beams_in,
    hits,
    select,
    picked,
    passing,
    rows_in,
    scored,
    half_out,
    block_out,
    half_left,
    half_right,
    block_left,
    block_right,
    total,
    returned,
    choose,
    columns,
    line,
    parent_out,
    parent_in,
    in_sem,
    w_sem,
    beam_send,
    beam_recv,
    z_send,
    z_recv,
    y_send,
    y_recv,
    via_send,
    via_recv,
    pass_send,
    fwd_send,
    fwd_recv,
    half_send,
    half_recv,
    block_send,
    block_recv,
    ret_send,
    ret_recv,
    parent_send,
    parent_recv,
):
    level = lax.axis_index("level")
    g = lax.axis_index("group")
    x = lax.axis_index("leaf")
    ny = ROWS_OF_CHIPS
    nz = groups // ny
    y, z = g // nz, g % nz
    right, left, across = (x + 1) % leaves, (x + leaves - 1) % leaves, (x + 2) % leaves
    fetched = 2 * (x % 2)
    other_two = 2 - fetched
    own_part = fetched + level
    beam_len, queries = beam_ref.shape
    feature, labels = w_ref.shape
    part = feature // leaves
    share = labels // leaves
    slots = groups * cap
    chunk = nz * cap
    half = chunk // 2

    copies = [
        pltpu.make_async_copy(src, dst, in_sem.at[n])
        for n, (src, dst) in enumerate(
            (
                (beam_hbm, beam_ref),
                (q_hbm, q_ref),
                (map_hbm, map_ref),
                (mask_hbm, mask_ref),
                (pos_hbm, pos_ref),
                (root_hbm, root_ref),
            )
        )
    ]
    for copy in copies:
        copy.start()
    weight_copy = pltpu.make_async_copy(w_ref, w_in, w_sem)
    weight_copy.start()

    barrier = pltpu.get_barrier_semaphore()

    def greet(o, carry):
        pl.semaphore_signal(
            barrier, inc=1, device_id={"group": (g + o) % groups}, device_id_type=MESH
        )
        return carry

    lax.fori_loop(1, groups, greet, 0)
    for other in (left, right):
        pl.semaphore_signal(barrier, inc=1, device_id={"leaf": other}, device_id_type=MESH)
    for n in range(1, leaves):
        pl.semaphore_signal(
            barrier,
            inc=1,
            device_id={"level": 1 - level, "leaf": (x + n) % leaves},
            device_id_type=MESH,
        )
    for n in range(nz):
        pl.semaphore_signal(
            barrier,
            inc=1,
            device_id={"level": 1 - level, "group": y * nz + (z + n) % nz},
            device_id_type=MESH,
        )
    for n in range(1, ny):
        pl.semaphore_signal(
            barrier,
            inc=1,
            device_id={"level": 1 - level, "group": ((y + n) % ny) * nz + z},
            device_id_type=MESH,
        )

    for copy in copies[:2]:
        copy.wait()
    beam = beam_ref[...]
    group_id = lax.broadcasted_iota(I32, (groups, queries), 0)
    hit = jnp.zeros((groups, queries), F32)
    for b in range(beam_len):
        hit = hit + (beam[b : b + 1, :] == group_id).astype(F32)
    earlier = (
        lax.broadcasted_iota(I32, (queries, queries), 0)
        < lax.broadcasted_iota(I32, (queries, queries), 1)
    ).astype(F32)
    rank = jnp.dot(hit.astype(BF16), earlier.astype(BF16), preferred_element_type=F32)
    place = group_id.astype(F32) * cap + rank
    slot = [
        jnp.sum(jnp.where(beam[b : b + 1, :] == group_id, place, 0.0), axis=0, keepdims=True)
        for b in range(beam_len)
    ]
    spread[0] = q_ref[:, pl.ds(pl.multiple_of(own_part * part, 128), part)]
    beams_own[...] = jnp.full_like(beams_own, -1)
    beams_own[:beam_len, :queries] = beam

    pl.semaphore_wait(barrier, groups - 1 + 2 + leaves - 1 + nz + ny - 1)

    def half_rows(which):
        return pl.ds(which * (queries // 2), queries // 2)

    def along_z(come, at, which, step):
        pltpu.make_async_remote_copy(
            src_ref=spread.at[come, half_rows(which)],
            dst_ref=spread.at[at, half_rows(which)],
            send_sem=z_send,
            recv_sem=z_recv.at[at, which],
            device_id={"group": y * nz + (z + nz + step) % nz},
            device_id_type=MESH,
        ).start()

    pltpu.make_async_copy(beams_own, beams_in.at[level * nz], beam_recv).start()
    for n in range(nz):
        at = 2 * n if n < nz // 2 else 2 * (nz - n) - 1
        for flip in range(2):
            if n or flip:
                pltpu.make_async_remote_copy(
                    src_ref=beams_own,
                    dst_ref=beams_in.at[level * nz + at],
                    send_sem=beam_send,
                    recv_sem=beam_recv,
                    device_id={
                        "level": (level + flip) % 2,
                        "group": y * nz + (z + n) % nz,
                    },
                    device_id_type=MESH,
                ).start()
    for which in range(2):
        along_z(0, 2, which, 1)
        along_z(0, 1, which, -1)

    wait_for(beams_in, beam_recv)
    eight = lax.broadcasted_iota(I32, (8, 128), 0)
    near_group = jnp.where(eight < ny, eight * nz + z, -2)

    def find_hits(n, carry):
        names = beams_in[n]
        found = jnp.zeros((8, 128), F32)
        for b in range(beam_len):
            found = found + (names[b : b + 1, :] == near_group).astype(F32)
        hits[pl.ds(pl.multiple_of(n * 8, 8), 8), :] = found
        return carry

    lax.fori_loop(0, 2 * nz, find_hits, 0)
    before = (
        lax.broadcasted_iota(I32, (128, 128), 0) < lax.broadcasted_iota(I32, (128, 128), 1)
    ).astype(F32)
    hits[...] = jnp.dot(
        hits[...].astype(BF16), before.astype(BF16), preferred_element_type=F32
    )
    near_slot = lax.broadcasted_iota(I32, (ny * cap, 128), 0).astype(F32)

    def make_select(n, carry):
        names = beams_in[n]
        place = eight.astype(F32) * cap + hits[pl.ds(pl.multiple_of(n * 8, 8), 8), :] + 1.0
        chosen = jnp.zeros((ny * cap, 128), F32)
        for b in range(beam_len):
            at = jnp.sum(
                jnp.where(names[b : b + 1, :] == near_group, place, 0.0), axis=0, keepdims=True
            )
            chosen = chosen + (at - 1.0 == near_slot).astype(F32)
        select[n % nz, pl.ds(pl.multiple_of((n // nz) * ny * cap, 16), ny * cap), :] = chosen.astype(
            BF16
        )
        return carry

    lax.fori_loop(0, 2 * nz, make_select, 0)

    blocks = cap // 8

    def slot_blocks(group):
        return pl.ds(group * blocks, blocks)

    def chunk_blocks(step):
        return pl.ds(step * (chunk // 8), chunk // 8)

    def distance_blocks(at):
        return pl.ds(at * (half // 8), half // 8)

    def pick(at):
        rows = jnp.dot(select[at, :, :queries], spread[at], preferred_element_type=F32)
        picked[at] = rows.astype(BF16).reshape(2, ny, blocks, 8, part)
        pltpu.make_async_copy(
            picked.at[at, level, y], rows_in.at[own_part, slot_blocks(at * ny + y)], y_recv.at[at // 2]
        ).start()
        for flip, step in ((0, 2), (1, 2), (0, 1), (0, 3), (1, 1), (1, 3), (1, 0)):
            to_level, to_row = (level + flip) % 2, (y + step) % ny
            pltpu.make_async_remote_copy(
                src_ref=picked.at[at, to_level, to_row],
                dst_ref=rows_in.at[own_part, slot_blocks(at * ny + y)],
                send_sem=y_send,
                recv_sem=y_recv.at[at // 2],
                device_id={"level": to_level, "group": to_row * nz + z},
                device_id_type=MESH,
            ).start()

    def pass_on(at):
        came_from = (y + (ny - 1 if at % 2 == 0 else 1)) % ny
        wait_for(passing.at[at], via_recv.at[at])
        for flip in range(2):
            to_level = (level + flip) % 2
            pltpu.make_async_remote_copy(
                src_ref=passing.at[at, to_level],
                dst_ref=rows_in.at[own_part, slot_blocks(at * ny + came_from)],
                send_sem=pass_send,
                recv_sem=y_recv.at[at // 2],
                device_id={"level": to_level, "group": ((came_from + 2) % ny) * nz + z},
                device_id_type=MESH,
            ).start()

    def to_leaf(src, dst, send, recv, other):
        pltpu.make_async_remote_copy(
            src_ref=src,
            dst_ref=dst,
            send_sem=send,
            recv_sem=recv,
            device_id={"leaf": other},
            device_id_type=MESH,
        ).start()

    def exchange(c):
        two = pl.ds(fetched, 2)
        wait_for(rows_in.at[two, chunk_blocks(c)], y_recv.at[c])
        for n, other in enumerate((right, left)):
            rows = rows_in.at[two, distance_blocks(2 * c + n)]
            to_leaf(rows, rows, fwd_send, fwd_recv.at[n, c], other)

    for copy in copies[2:]:
        copy.wait()
    tile, tall = 256, 1024
    mask_rows = feature // mask_ref.shape[0]

    def fill_perm(n, carry):
        at = pl.ds(pl.multiple_of(n * tile, tile), tile)
        column = lax.broadcasted_iota(I32, (tile, labels), 0) + n * tile
        perm[at, :] = (column == map_ref[...]).astype(F32).astype(BF16)
        return carry

    lax.fori_loop(0, labels // tile, fill_perm, 0)
    weight_copy.wait()

    def permute(n, carry):
        row = n // (labels // tile)
        at = pl.ds(pl.multiple_of((n % (labels // tile)) * tile, tile), tile)
        product = jnp.dot(
            w_in[pl.ds(pl.multiple_of(row * tall, tall), tall), :],
            perm[:, at],
            preferred_element_type=F32,
        )
        for m in range(tall // mask_rows):
            keep = mask_ref[row * (tall // mask_rows) + m].astype(F32)
            w_own[pl.ds(pl.multiple_of(row * tall + m * mask_rows, mask_rows), mask_rows), at] = (
                product[m * mask_rows : (m + 1) * mask_rows] * keep
            ).astype(BF16)
        return carry

    tiles = (feature // tall) * (labels // tile)
    pick(0)
    for hop in range(1, ny):
        up, down = 2 * hop, 2 * hop - 1
        for which in range(2):
            wait_for(spread.at[up, half_rows(which)], z_recv.at[up, which])
            if hop < ny - 1 or which == 0:
                along_z(up, min(up + 2, nz - 1), which, 1)
            wait_for(spread.at[down, half_rows(which)], z_recv.at[down, which])
            if hop < ny - 1 or which == 1:
                along_z(down, down + 2, which, -1)
        pick(down)
        pick(up)
        lax.fori_loop(tiles * (hop - 1) // ny, tiles * hop // ny, permute, 0)
        if hop == ny - 1:
            exchange(0)
    for which in range(2):
        wait_for(spread.at[nz - 1, half_rows(which)], z_recv.at[nz - 1, which])
    pick(nz - 1)
    exchange(1)
    lax.fori_loop(tiles * (ny - 1) // ny, tiles, permute, 0)

    pos = pos_ref[...]
    parent_slot, parent_label = pos // labels, (pos % labels).astype(F32)
    root = root_ref[...].astype(F32)
    line[...] = jnp.zeros_like(line)
    for b in range(beam_len):
        line[b : b + 1, :queries] = slot[b]
        line[2 * beam_len + b : 2 * beam_len + b + 1, :queries] = parent_label[b : b + 1]
        line[3 * beam_len + b : 3 * beam_len + b + 1, :queries] = root[b : b + 1]
        slot_of = jnp.zeros((1, queries), F32)
        root_of = jnp.zeros((1, queries), F32)
        for s in range(beam_len):
            same = parent_slot[b : b + 1] == s
            slot_of = slot_of + jnp.where(same, slot[s], 0.0)
            root_of = root_of + jnp.where(same, root[s : s + 1], 0.0)
        line[beam_len + b : beam_len + b + 1, :queries] = slot_of
        line[4 * beam_len + b : 4 * beam_len + b + 1, :queries] = root_of
    columns[...] = jnp.transpose(line[...])
    across_slots = lax.broadcasted_iota(I32, (queries, slots), 1).astype(F32)
    for b in range(2 * beam_len):
        choose[b * queries : (b + 1) * queries, :] = (
            (columns[:queries, b : b + 1] == across_slots).astype(F32).astype(BF16)
        )

    def stage(t, carry):
        @pl.when(t < 2)
        def _():
            exchange(t + ny - 2)

        @pl.when(t < ny)
        def _():
            c = t
            two = pl.ds(other_two, 2)
            for n in range(2):
                wait_for(rows_in.at[two, distance_blocks(2 * c + n)], fwd_recv.at[n, c])

            logits = jnp.zeros((chunk, labels), F32)
            for p in range(leaves):
                logits = logits + jnp.dot(
                    rows_in[p, chunk_blocks(c)].reshape(chunk, part),
                    w_own[p * part : (p + 1) * part, :],
                    preferred_element_type=F32,
                )
            one_tree = jax.nn.sigmoid(logits)
            for j in range(leaves):
                scored[c, j] = one_tree[:, j * share : (j + 1) * share]
            half_out[c] = encode(scored[c, across])
            to_leaf(
                half_out.at[c, pl.ds(0, half)],
                half_left.at[c],
                half_send,
                half_recv.at[0, c],
                right,
            )
            to_leaf(
                half_out.at[c, pl.ds(half, half)],
                half_right.at[c],
                half_send,
                half_recv.at[1, c],
                left,
            )

        @pl.when((t >= 1) & (t < ny + 1))
        def _():
            c = t - 1
            wait_for(half_left.at[c], half_recv.at[0, c])
            block_out[c, 0, :half] = encode(scored[c, right, :half] + decode(half_left[c]))
            block_out[c, 0, half:] = encode(scored[c, right, half:])
            to_leaf(
                block_out.at[c, 0], block_left.at[c], block_send, block_recv.at[0, c], right
            )
            wait_for(half_right.at[c], half_recv.at[1, c])
            block_out[c, 1, :half] = encode(scored[c, left, :half])
            block_out[c, 1, half:] = encode(scored[c, left, half:] + decode(half_right[c]))
            to_leaf(
                block_out.at[c, 1], block_right.at[c], block_send, block_recv.at[1, c], left
            )

        @pl.when(t >= 2)
        def _():
            c = t - 2
            wait_for(block_left.at[c], block_recv.at[0, c])
            wait_for(block_right.at[c], block_recv.at[1, c])
            sums = scored[c, x] + (decode(block_left[c]) + decode(block_right[c]))
            total[c] = encode(sums.reshape(chunk // 8, 8, share))

            def send_back(n, carry):
                row = (y + n) % ny
                place = jnp.where(n < ny, z + nz - c, z + c + 1) % nz
                pltpu.make_async_remote_copy(
                    src_ref=total.at[c, slot_blocks((n // ny) * ny + row)],
                    dst_ref=returned.at[slot_blocks(g)],
                    send_sem=ret_send,
                    recv_sem=ret_recv,
                    device_id={"group": row * nz + place},
                    device_id_type=MESH,
                ).start()
                return carry

            @pl.when(c == 0)
            def _():
                pltpu.make_async_copy(
                    total.at[c, slot_blocks(y)], returned.at[slot_blocks(g)], ret_recv
                ).start()

            @pl.when(c > 0)
            def _():
                send_back(0, 0)

            lax.fori_loop(1, 2 * ny, send_back, 0)

        return carry

    lax.fori_loop(0, ny + 2, stage, 0)

    wait_for(returned, ret_recv)
    high, low = two_parts(decode(returned[...]).reshape(slots, share))
    entries = beam_len * queries

    def gather(at):
        chosen = choose[at, :]
        return jnp.dot(chosen, high, preferred_element_type=F32) + jnp.dot(
            chosen, low, preferred_element_type=F32
        )

    def to_level_one(other, carry):
        pltpu.make_async_remote_copy(
            src_ref=parent_out,
            dst_ref=parent_in.at[x],
            send_sem=parent_send,
            recv_sem=parent_recv,
            device_id={"level": 1, "leaf": other},
            device_id_type=MESH,
        ).start()
        return carry

    @pl.when(level == 0)
    def _():
        lane = lax.broadcasted_iota(I32, (queries, share), 1).astype(F32) + (x * share).astype(F32)
        wide = lax.broadcasted_iota(I32, (queries, 128), 1)
        sums = gather(slice(entries, 2 * entries))
        parents = jnp.zeros((queries, 128), F32)
        for b in range(beam_len):
            at_label = columns[:queries, 2 * beam_len + b : 2 * beam_len + b + 1] == lane
            mine = jnp.where(at_label, sums[b * queries : (b + 1) * queries], 0.0)
            value = jnp.sum(mine, axis=1, keepdims=True) * columns[
                :queries, 4 * beam_len + b : 4 * beam_len + b + 1
            ]
            parents = jnp.where(wide == b, value, parents)
        parent_out[...] = parents
        lax.fori_loop(0, leaves, to_level_one, 0)

    sums = gather(slice(0, entries))

    @pl.when(level == 0)
    def _():
        for b in range(beam_len):
            out_ref[b] = (
                sums[b * queries : (b + 1) * queries]
                * columns[:queries, 3 * beam_len + b : 3 * beam_len + b + 1]
            )

        wait_for(parent_in, parent_send)

    @pl.when(level == 1)
    def _():
        wait_for(parent_in, parent_recv)
        parents = parent_in[0]
        for n in range(1, leaves):
            parents = parents + parent_in[n]
        parents = (parents / leaves).astype(BF16).astype(F32)
        for b in range(beam_len):
            out_ref[b] = sums[b * queries : (b + 1) * queries] * parents[:, b : b + 1]

    wait_for(beams_in.at[pl.ds(0, 2 * nz - 1)], beam_send)
    wait_for(spread.at[pl.ds(0, nz - 1)], z_send)
    wait_for(picked.at[pl.ds(0, 7)], y_send)
    wait_for(rows_in.at[pl.ds(0, 2)], fwd_send)
    wait_for(half_out, half_send)
    wait_for(block_out, block_send)
    wait_for(returned.at[pl.ds(0, (groups - 1) * cap // 8)], ret_send)


def body(queries, weights, block_mask, label_map, beam_lists, root_score, parent_pos):
    groups, leaves = lax.axis_size("group"), lax.axis_size("leaf")
    rows, feature = queries.shape
    labels = weights.shape[4]
    beam_len = beam_lists.shape[2]
    cap = rows // QBLK * CAP
    slots = groups * cap
    ny = ROWS_OF_CHIPS
    nz = groups // ny
    chunk = slots // ny
    half = chunk // 2
    share = labels // leaves
    vmem = pl.BlockSpec(memory_space=pltpu.VMEM)
    dma = pltpu.SemaphoreType.DMA
    out = pl.pallas_call(
        functools.partial(kernel, groups, leaves, cap),
        out_shape=jax.ShapeDtypeStruct((beam_len, rows, share), F32),
        in_specs=[pl.BlockSpec(memory_space=pltpu.HBM)] * 7,
        out_specs=vmem,
        scratch_shapes=[
            pltpu.VMEM((rows, feature), BF16),
            pltpu.SMEM((block_mask.shape[3],), I32),
            pltpu.VMEM((1, labels), I32),
            pltpu.VMEM((beam_len, rows), I32),
            pltpu.VMEM((beam_len, rows), BF16),
            pltpu.VMEM((beam_len, rows), I32),
            pltpu.VMEM((feature, labels), BF16),
            pltpu.VMEM((feature, labels), BF16),
            pltpu.VMEM((labels, labels), BF16),
            pltpu.VMEM((nz, rows, feature // leaves), BF16),
            pltpu.VMEM((8, 128), I32),
            pltpu.VMEM((2 * nz, 8, 128), I32),
            pltpu.VMEM((16 * nz, 128), F32),
            pltpu.VMEM((nz, chunk, 128), BF16),
            pltpu.VMEM((nz, 2, ny, cap // 8, 8, feature // leaves), BF16),
            pltpu.VMEM((nz, 2, cap // 8, 8, feature // leaves), BF16),
            pltpu.VMEM((leaves, slots // 8, 8, feature // leaves), BF16),
            pltpu.VMEM((ny, leaves, chunk, share), F32),
            pltpu.VMEM((ny, chunk, share), I16),
            pltpu.VMEM((ny, 2, chunk, share), I16),
            pltpu.VMEM((ny, half, share), I16),
            pltpu.VMEM((ny, half, share), I16),
            pltpu.VMEM((ny, chunk, share), I16),
            pltpu.VMEM((ny, chunk, share), I16),
            pltpu.VMEM((ny, chunk // 8, 8, share), I16),
            pltpu.VMEM((slots // 8, 8, share), I16),
            pltpu.VMEM((2 * beam_len * rows, slots), BF16),
            pltpu.VMEM((128, 128), F32),
            pltpu.VMEM((128, 128), F32),
            pltpu.VMEM((rows, 128), F32),
            pltpu.VMEM((leaves, rows, 128), F32),
            dma((6,)),
            dma,
            dma,
            dma,
            dma,
            dma((nz, 2)),
            dma,
            dma((ny,)),
            dma,
            dma((nz,)),
            dma,
            dma,
            dma((2, ny)),
            dma,
            dma((2, ny)),
            dma,
            dma((2, ny)),
            dma,
            dma,
            dma,
            dma,
        ],
        compiler_params=pltpu.CompilerParams(
            collective_id=0, has_side_effects=True, vmem_limit_bytes=60 << 20
        ),
    )(
        queries,
        weights[0, 0, 0],
        block_mask[0, 0, 0],
        label_map[0, 0],
        beam_lists[0].T,
        root_score.T,
        parent_pos.T,
    )
    return jnp.transpose(out, (1, 0, 2))[None]


def solution(mesh):
    in_specs = (
        P("group", None),
        P("level", "leaf", "group", None, None),
        P("level", "leaf", "group", None),
        P("level", "leaf", "group", None),
        P("level", "group", None),
        P("group", None),
        P("group", None),
    )
    out_specs = P("level", "group", None, "leaf")
    return jax.shard_map(body, mesh=mesh, in_specs=in_specs, out_specs=out_specs, check_vma=False)
```

```python
import functools

import jax
import jax.numpy as jnp
from jax import lax
from jax.experimental import pallas as pl
from jax.experimental.pallas import tpu as pltpu
from jax.sharding import PartitionSpec as P

QBLK = 32
CAP = 8
ROWS_OF_CHIPS = 4
MESH = pl.DeviceIdType.MESH
F32, BF16, I32, I16 = jnp.float32, jnp.bfloat16, jnp.int32, jnp.int16


def encode(value):
    octaves = jnp.log2(jnp.maximum(value, 2.0**-61))
    return jnp.round((octaves + 29.0) * 1024.0).astype(I32).astype(I16)


def decode(code):
    return jnp.exp2(code.astype(I32).astype(F32) * (1.0 / 1024.0) - 29.0)


def two_parts(value):
    high = value.astype(BF16)
    return high, (value - high.astype(F32)).astype(BF16)


def wait_for(ref, sem):
    pltpu.make_async_copy(ref, ref, sem).wait()


def kernel(
    groups,
    leaves,
    cap,
    q_hbm,
    w_ref,
    mask_hbm,
    map_hbm,
    beam_hbm,
    root_hbm,
    pos_hbm,
    out_ref,
    q_ref,
    mask_ref,
    map_ref,
    beam_ref,
    root_ref,
    pos_ref,
    w_in,
    w_own,
    perm,
    spread,
    beams_own,
    beams_in,
    hits,
    select,
    picked,
    rows_in,
    scored,
    half_out,
    block_out,
    half_left,
    half_right,
    block_left,
    block_right,
    total,
    returned,
    choose,
    columns,
    line,
    parent_out,
    parent_in,
    in_sem,
    w_sem,
    beam_send,
    beam_recv,
    z_send,
    z_recv,
    y_send,
    y_recv,
    fwd_send,
    fwd_recv,
    half_send,
    half_recv,
    block_send,
    block_recv,
    ret_send,
    ret_recv,
    parent_send,
    parent_recv,
):
    level = lax.axis_index("level")
    g = lax.axis_index("group")
    x = lax.axis_index("leaf")
    ny = ROWS_OF_CHIPS
    nz = groups // ny
    y, z = g // nz, g % nz
    right, left, across = (x + 1) % leaves, (x + leaves - 1) % leaves, (x + 2) % leaves
    fetched = 2 * (x % 2)
    other_two = 2 - fetched
    own_part = fetched + level
    beam_len, queries = beam_ref.shape
    feature, labels = w_ref.shape
    part = feature // leaves
    share = labels // leaves
    slots = groups * cap
    chunk = nz * cap
    half = chunk // 2

    copies = [
        pltpu.make_async_copy(src, dst, in_sem.at[n])
        for n, (src, dst) in enumerate(
            (
                (beam_hbm, beam_ref),
                (q_hbm, q_ref),
                (map_hbm, map_ref),
                (mask_hbm, mask_ref),
                (pos_hbm, pos_ref),
                (root_hbm, root_ref),
            )
        )
    ]
    for copy in copies:
        copy.start()
    weight_copy = pltpu.make_async_copy(w_ref, w_in, w_sem)
    weight_copy.start()

    barrier = pltpu.get_barrier_semaphore()

    def greet(o, carry):
        pl.semaphore_signal(
            barrier, inc=1, device_id={"group": (g + o) % groups}, device_id_type=MESH
        )
        return carry

    lax.fori_loop(1, groups, greet, 0)
    for other in (left, right):
        pl.semaphore_signal(barrier, inc=1, device_id={"leaf": other}, device_id_type=MESH)
    for n in range(1, leaves):
        pl.semaphore_signal(
            barrier,
            inc=1,
            device_id={"level": 1 - level, "leaf": (x + n) % leaves},
            device_id_type=MESH,
        )
    for n in range(nz):
        pl.semaphore_signal(
            barrier,
            inc=1,
            device_id={"level": 1 - level, "group": y * nz + (z + n) % nz},
            device_id_type=MESH,
        )
    for n in range(1, ny):
        pl.semaphore_signal(
            barrier,
            inc=1,
            device_id={"level": 1 - level, "group": ((y + n) % ny) * nz + z},
            device_id_type=MESH,
        )

    for copy in copies[:2]:
        copy.wait()
    beam = beam_ref[...]
    group_id = lax.broadcasted_iota(I32, (groups, queries), 0)
    hit = jnp.zeros((groups, queries), F32)
    for b in range(beam_len):
        hit = hit + (beam[b : b + 1, :] == group_id).astype(F32)
    earlier = (
        lax.broadcasted_iota(I32, (queries, queries), 0)
        < lax.broadcasted_iota(I32, (queries, queries), 1)
    ).astype(F32)
    rank = jnp.dot(hit.astype(BF16), earlier.astype(BF16), preferred_element_type=F32)
    place = group_id.astype(F32) * cap + rank
    slot = [
        jnp.sum(jnp.where(beam[b : b + 1, :] == group_id, place, 0.0), axis=0, keepdims=True)
        for b in range(beam_len)
    ]
    spread[0] = q_ref[:, pl.ds(pl.multiple_of(own_part * part, 128), part)]
    beams_own[...] = jnp.full_like(beams_own, -1)
    beams_own[:beam_len, :queries] = beam

    pl.semaphore_wait(barrier, groups - 1 + 2 + leaves - 1 + nz + ny - 1)

    def half_rows(which):
        return pl.ds(which * (queries // 2), queries // 2)

    def along_z(come, at, step, which=None):
        rows = pl.ds(0, queries) if which is None else half_rows(which)
        pltpu.make_async_remote_copy(
            src_ref=spread.at[come, rows],
            dst_ref=spread.at[at, rows],
            send_sem=z_send,
            recv_sem=z_recv.at[at],
            device_id={"group": y * nz + (z + nz + step) % nz},
            device_id_type=MESH,
        ).start()

    def from_z(at):
        wait_for(spread.at[at], z_recv.at[at])

    pltpu.make_async_copy(beams_own, beams_in.at[level * nz], beam_recv).start()
    for n in range(nz):
        at = 2 * n if n < nz // 2 else 2 * (nz - n) - 1
        for flip in range(2):
            if n or flip:
                pltpu.make_async_remote_copy(
                    src_ref=beams_own,
                    dst_ref=beams_in.at[level * nz + at],
                    send_sem=beam_send,
                    recv_sem=beam_recv,
                    device_id={
                        "level": (level + flip) % 2,
                        "group": y * nz + (z + n) % nz,
                    },
                    device_id_type=MESH,
                ).start()
    along_z(0, 2, 1)
    along_z(0, 1, -1)
    along_z(0, 4, 2)
    along_z(0, 3, -2)

    wait_for(beams_in, beam_recv)
    eight = lax.broadcasted_iota(I32, (8, 128), 0)
    near_group = jnp.where(eight < ny, eight * nz + z, -2)

    def find_hits(n, carry):
        names = beams_in[n]
        found = jnp.zeros((8, 128), F32)
        for b in range(beam_len):
            found = found + (names[b : b + 1, :] == near_group).astype(F32)
        hits[pl.ds(pl.multiple_of(n * 8, 8), 8), :] = found
        return carry

    lax.fori_loop(0, 2 * nz, find_hits, 0)
    before = (
        lax.broadcasted_iota(I32, (128, 128), 0) < lax.broadcasted_iota(I32, (128, 128), 1)
    ).astype(F32)
    hits[...] = jnp.dot(
        hits[...].astype(BF16), before.astype(BF16), preferred_element_type=F32
    )
    near_slot = lax.broadcasted_iota(I32, (ny * cap, 128), 0).astype(F32)

    def make_select(n, carry):
        names = beams_in[n]
        place = eight.astype(F32) * cap + hits[pl.ds(pl.multiple_of(n * 8, 8), 8), :] + 1.0
        chosen = jnp.zeros((ny * cap, 128), F32)
        for b in range(beam_len):
            at = jnp.sum(
                jnp.where(names[b : b + 1, :] == near_group, place, 0.0), axis=0, keepdims=True
            )
            chosen = chosen + (at - 1.0 == near_slot).astype(F32)
        select[n % nz, pl.ds(pl.multiple_of((n // nz) * ny * cap, 16), ny * cap), :] = chosen.astype(
            BF16
        )
        return carry

    lax.fori_loop(0, 2 * nz, make_select, 0)

    blocks = cap // 8

    def slot_blocks(group):
        return pl.ds(group * blocks, blocks)

    def chunk_blocks(step):
        return pl.ds(step * (chunk // 8), chunk // 8)

    def distance_blocks(at):
        return pl.ds(at * (half // 8), half // 8)

    def pick(at):
        rows = jnp.dot(select[at, :, :queries], spread[at], preferred_element_type=F32)
        picked[at] = rows.astype(BF16).reshape(2, ny, blocks, 8, part)
        pltpu.make_async_copy(
            picked.at[at, level, y], rows_in.at[own_part, slot_blocks(at * ny + y)], y_recv.at[at // 2]
        ).start()
        for flip, step in ((0, 2), (1, 2), (0, 1), (0, 3), (1, 1), (1, 3), (1, 0)):
            to_level, to_row = (level + flip) % 2, (y + step) % ny
            pltpu.make_async_remote_copy(
                src_ref=picked.at[at, to_level, to_row],
                dst_ref=rows_in.at[own_part, slot_blocks(at * ny + y)],
                send_sem=y_send,
                recv_sem=y_recv.at[at // 2],
                device_id={"level": to_level, "group": to_row * nz + z},
                device_id_type=MESH,
            ).start()

    def to_leaf(src, dst, send, recv, other):
        pltpu.make_async_remote_copy(
            src_ref=src,
            dst_ref=dst,
            send_sem=send,
            recv_sem=recv,
            device_id={"leaf": other},
            device_id_type=MESH,
        ).start()

    def exchange(c):
        two = pl.ds(fetched, 2)
        wait_for(rows_in.at[two, chunk_blocks(c)], y_recv.at[c])
        for n, other in enumerate((right, left)):
            rows = rows_in.at[two, distance_blocks(2 * c + n)]
            to_leaf(rows, rows, fwd_send, fwd_recv.at[n, c], other)

    for copy in copies[2:]:
        copy.wait()
    tile, tall = 256, 1024
    mask_rows = feature // mask_ref.shape[0]

    def fill_perm(n, carry):
        at = pl.ds(pl.multiple_of(n * tile, tile), tile)
        column = lax.broadcasted_iota(I32, (tile, labels), 0) + n * tile
        perm[at, :] = (column == map_ref[...]).astype(F32).astype(BF16)
        return carry

    lax.fori_loop(0, labels // tile, fill_perm, 0)
    weight_copy.wait()

    def permute(n, carry):
        row = n // (labels // tile)
        at = pl.ds(pl.multiple_of((n % (labels // tile)) * tile, tile), tile)
        product = jnp.dot(
            w_in[pl.ds(pl.multiple_of(row * tall, tall), tall), :],
            perm[:, at],
            preferred_element_type=F32,
        )
        for m in range(tall // mask_rows):
            keep = mask_ref[row * (tall // mask_rows) + m].astype(F32)
            w_own[pl.ds(pl.multiple_of(row * tall + m * mask_rows, mask_rows), mask_rows), at] = (
                product[m * mask_rows : (m + 1) * mask_rows] * keep
            ).astype(BF16)
        return carry

    tiles = (feature // tall) * (labels // tile)
    def permute_part(n):
        lax.fori_loop(tiles * n // ny, tiles * (n + 1) // ny, permute, 0)

    pick(0)
    for at in (1, 2):
        from_z(at)
        pick(at)
    permute_part(0)
    from_z(4)
    along_z(4, 6, 1)
    along_z(4, 7, 2, 0)
    from_z(3)
    along_z(3, 5, -1)
    along_z(3, 7, -2, 1)
    pick(3)
    pick(4)
    permute_part(1)
    exchange(0)
    permute_part(2)
    for at in (5, 6):
        from_z(at)
        pick(at)
    exchange(1)
    from_z(7)
    pick(7)
    permute_part(3)

    pos = pos_ref[...]
    parent_slot, parent_label = pos // labels, (pos % labels).astype(F32)
    root = root_ref[...].astype(F32)
    line[...] = jnp.zeros_like(line)
    for b in range(beam_len):
        line[b : b + 1, :queries] = slot[b]
        line[2 * beam_len + b : 2 * beam_len + b + 1, :queries] = parent_label[b : b + 1]
        line[3 * beam_len + b : 3 * beam_len + b + 1, :queries] = root[b : b + 1]
        slot_of = jnp.zeros((1, queries), F32)
        root_of = jnp.zeros((1, queries), F32)
        for s in range(beam_len):
            same = parent_slot[b : b + 1] == s
            slot_of = slot_of + jnp.where(same, slot[s], 0.0)
            root_of = root_of + jnp.where(same, root[s : s + 1], 0.0)
        line[beam_len + b : beam_len + b + 1, :queries] = slot_of
        line[4 * beam_len + b : 4 * beam_len + b + 1, :queries] = root_of
    columns[...] = jnp.transpose(line[...])
    across_slots = lax.broadcasted_iota(I32, (queries, slots), 1).astype(F32)
    for b in range(2 * beam_len):
        choose[b * queries : (b + 1) * queries, :] = (
            (columns[:queries, b : b + 1] == across_slots).astype(F32).astype(BF16)
        )

    def stage(t, carry):
        @pl.when(t < 2)
        def _():
            exchange(t + ny - 2)

        @pl.when(t < ny)
        def _():
            c = t
            two = pl.ds(other_two, 2)
            for n in range(2):
                wait_for(rows_in.at[two, distance_blocks(2 * c + n)], fwd_recv.at[n, c])

            logits = jnp.zeros((chunk, labels), F32)
            for p in range(leaves):
                logits = logits + jnp.dot(
                    rows_in[p, chunk_blocks(c)].reshape(chunk, part),
                    w_own[p * part : (p + 1) * part, :],
                    preferred_element_type=F32,
                )
            one_tree = jax.nn.sigmoid(logits)
            for j in range(leaves):
                scored[c, j] = one_tree[:, j * share : (j + 1) * share]
            half_out[c] = encode(scored[c, across])
            to_leaf(
                half_out.at[c, pl.ds(0, half)],
                half_left.at[c],
                half_send,
                half_recv.at[0, c],
                right,
            )
            to_leaf(
                half_out.at[c, pl.ds(half, half)],
                half_right.at[c],
                half_send,
                half_recv.at[1, c],
                left,
            )

        @pl.when((t >= 1) & (t < ny + 1))
        def _():
            c = t - 1
            wait_for(half_left.at[c], half_recv.at[0, c])
            block_out[c, 0, :half] = encode(scored[c, right, :half] + decode(half_left[c]))
            block_out[c, 0, half:] = encode(scored[c, right, half:])
            to_leaf(
                block_out.at[c, 0], block_left.at[c], block_send, block_recv.at[0, c], right
            )
            wait_for(half_right.at[c], half_recv.at[1, c])
            block_out[c, 1, :half] = encode(scored[c, left, :half])
            block_out[c, 1, half:] = encode(scored[c, left, half:] + decode(half_right[c]))
            to_leaf(
                block_out.at[c, 1], block_right.at[c], block_send, block_recv.at[1, c], left
            )

        @pl.when(t >= 2)
        def _():
            c = t - 2
            wait_for(block_left.at[c], block_recv.at[0, c])
            wait_for(block_right.at[c], block_recv.at[1, c])
            sums = scored[c, x] + (decode(block_left[c]) + decode(block_right[c]))
            total[c] = encode(sums.reshape(chunk // 8, 8, share))

            def send_back(n, carry):
                row = (y + n) % ny
                place = jnp.where(n < ny, z + nz - c, z + c + 1) % nz
                pltpu.make_async_remote_copy(
                    src_ref=total.at[c, slot_blocks((n // ny) * ny + row)],
                    dst_ref=returned.at[slot_blocks(g)],
                    send_sem=ret_send,
                    recv_sem=ret_recv,
                    device_id={"group": row * nz + place},
                    device_id_type=MESH,
                ).start()
                return carry

            @pl.when(c == 0)
            def _():
                pltpu.make_async_copy(
                    total.at[c, slot_blocks(y)], returned.at[slot_blocks(g)], ret_recv
                ).start()

            @pl.when(c > 0)
            def _():
                send_back(0, 0)

            lax.fori_loop(1, 2 * ny, send_back, 0)

        return carry

    lax.fori_loop(0, ny + 2, stage, 0)

    wait_for(returned, ret_recv)
    high, low = two_parts(decode(returned[...]).reshape(slots, share))
    entries = beam_len * queries

    def gather(at):
        chosen = choose[at, :]
        return jnp.dot(chosen, high, preferred_element_type=F32) + jnp.dot(
            chosen, low, preferred_element_type=F32
        )

    def to_level_one(other, carry):
        pltpu.make_async_remote_copy(
            src_ref=parent_out,
            dst_ref=parent_in.at[x],
            send_sem=parent_send,
            recv_sem=parent_recv,
            device_id={"level": 1, "leaf": other},
            device_id_type=MESH,
        ).start()
        return carry

    @pl.when(level == 0)
    def _():
        lane = lax.broadcasted_iota(I32, (queries, share), 1).astype(F32) + (x * share).astype(F32)
        wide = lax.broadcasted_iota(I32, (queries, 128), 1)
        sums = gather(slice(entries, 2 * entries))
        parents = jnp.zeros((queries, 128), F32)
        for b in range(beam_len):
            at_label = columns[:queries, 2 * beam_len + b : 2 * beam_len + b + 1] == lane
            mine = jnp.where(at_label, sums[b * queries : (b + 1) * queries], 0.0)
            value = jnp.sum(mine, axis=1, keepdims=True) * columns[
                :queries, 4 * beam_len + b : 4 * beam_len + b + 1
            ]
            parents = jnp.where(wide == b, value, parents)
        parent_out[...] = parents
        lax.fori_loop(0, leaves, to_level_one, 0)

    sums = gather(slice(0, entries))

    @pl.when(level == 0)
    def _():
        for b in range(beam_len):
            out_ref[b] = (
                sums[b * queries : (b + 1) * queries]
                * columns[:queries, 3 * beam_len + b : 3 * beam_len + b + 1]
            )

        wait_for(parent_in, parent_send)

    @pl.when(level == 1)
    def _():
        wait_for(parent_in, parent_recv)
        parents = parent_in[0]
        for n in range(1, leaves):
            parents = parents + parent_in[n]
        parents = (parents / leaves).astype(BF16).astype(F32)
        for b in range(beam_len):
            out_ref[b] = sums[b * queries : (b + 1) * queries] * parents[:, b : b + 1]

    wait_for(beams_in.at[pl.ds(0, 2 * nz - 1)], beam_send)
    wait_for(spread.at[pl.ds(0, nz - 1)], z_send)
    wait_for(picked.at[pl.ds(0, 7)], y_send)
    wait_for(rows_in.at[pl.ds(0, 2)], fwd_send)
    wait_for(half_out, half_send)
    wait_for(block_out, block_send)
    wait_for(returned.at[pl.ds(0, (groups - 1) * cap // 8)], ret_send)


def body(queries, weights, block_mask, label_map, beam_lists, root_score, parent_pos):
    groups, leaves = lax.axis_size("group"), lax.axis_size("leaf")
    rows, feature = queries.shape
    labels = weights.shape[4]
    beam_len = beam_lists.shape[2]
    cap = rows // QBLK * CAP
    slots = groups * cap
    ny = ROWS_OF_CHIPS
    nz = groups // ny
    chunk = slots // ny
    half = chunk // 2
    share = labels // leaves
    vmem = pl.BlockSpec(memory_space=pltpu.VMEM)
    dma = pltpu.SemaphoreType.DMA
    out = pl.pallas_call(
        functools.partial(kernel, groups, leaves, cap),
        out_shape=jax.ShapeDtypeStruct((beam_len, rows, share), F32),
        in_specs=[pl.BlockSpec(memory_space=pltpu.HBM)] * 7,
        out_specs=vmem,
        scratch_shapes=[
            pltpu.VMEM((rows, feature), BF16),
            pltpu.SMEM((block_mask.shape[3],), I32),
            pltpu.VMEM((1, labels), I32),
            pltpu.VMEM((beam_len, rows), I32),
            pltpu.VMEM((beam_len, rows), BF16),
            pltpu.VMEM((beam_len, rows), I32),
            pltpu.VMEM((feature, labels), BF16),
            pltpu.VMEM((feature, labels), BF16),
            pltpu.VMEM((labels, labels), BF16),
            pltpu.VMEM((nz, rows, feature // leaves), BF16),
            pltpu.VMEM((8, 128), I32),
            pltpu.VMEM((2 * nz, 8, 128), I32),
            pltpu.VMEM((16 * nz, 128), F32),
            pltpu.VMEM((nz, chunk, 128), BF16),
            pltpu.VMEM((nz, 2, ny, cap // 8, 8, feature // leaves), BF16),
            pltpu.VMEM((leaves, slots // 8, 8, feature // leaves), BF16),
            pltpu.VMEM((ny, leaves, chunk, share), F32),
            pltpu.VMEM((ny, chunk, share), I16),
            pltpu.VMEM((ny, 2, chunk, share), I16),
            pltpu.VMEM((ny, half, share), I16),
            pltpu.VMEM((ny, half, share), I16),
            pltpu.VMEM((ny, chunk, share), I16),
            pltpu.VMEM((ny, chunk, share), I16),
            pltpu.VMEM((ny, chunk // 8, 8, share), I16),
            pltpu.VMEM((slots // 8, 8, share), I16),
            pltpu.VMEM((2 * beam_len * rows, slots), BF16),
            pltpu.VMEM((128, 128), F32),
            pltpu.VMEM((128, 128), F32),
            pltpu.VMEM((rows, 128), F32),
            pltpu.VMEM((leaves, rows, 128), F32),
            dma((6,)),
            dma,
            dma,
            dma,
            dma,
            dma((nz,)),
            dma,
            dma((ny,)),
            dma,
            dma((2, ny)),
            dma,
            dma((2, ny)),
            dma,
            dma((2, ny)),
            dma,
            dma,
            dma,
            dma,
        ],
        compiler_params=pltpu.CompilerParams(
            collective_id=0, has_side_effects=True, vmem_limit_bytes=52 << 20
        ),
    )(
        *(
            pltpu.with_memory_space_constraint(operand, pltpu.HBM)
            for operand in (
                queries,
                weights[0, 0, 0],
                block_mask[0, 0, 0],
                label_map[0, 0],
                beam_lists[0].T,
                root_score.T,
                parent_pos.T,
            )
        )
    )
    return jnp.transpose(out, (1, 0, 2))[None]


def solution(mesh):
    in_specs = (
        P("group", None),
        P("level", "leaf", "group", None, None),
        P("level", "leaf", "group", None),
        P("level", "leaf", "group", None),
        P("level", "group", None),
        P("group", None),
        P("group", None),
    )
    out_specs = P("level", "group", None, "leaf")
    return jax.shard_map(body, mesh=mesh, in_specs=in_specs, out_specs=out_specs, check_vma=False)
```

```python
import functools

import jax
import jax.numpy as jnp
from jax import lax
from jax.experimental import pallas as pl
from jax.experimental.pallas import tpu as pltpu
from jax.sharding import PartitionSpec as P

QBLK = 32
CAP = 8
ROWS_OF_CHIPS = 4
MESH = pl.DeviceIdType.MESH
F32, BF16, I32, I16 = jnp.float32, jnp.bfloat16, jnp.int32, jnp.int16


def encode(value):
    octaves = jnp.log2(jnp.maximum(value, 2.0**-61))
    return jnp.round((octaves + 29.0) * 1024.0).astype(I32).astype(I16)


def decode(code):
    return jnp.exp2(code.astype(I32).astype(F32) * (1.0 / 1024.0) - 29.0)


def two_parts(value):
    high = value.astype(BF16)
    return high, (value - high.astype(F32)).astype(BF16)


def wait_for(ref, sem):
    pltpu.make_async_copy(ref, ref, sem).wait()


def kernel(
    groups,
    leaves,
    cap,
    q_hbm,
    w_ref,
    mask_hbm,
    map_hbm,
    beam_hbm,
    root_hbm,
    pos_hbm,
    out_ref,
    q_ref,
    mask_ref,
    map_ref,
    beam_ref,
    root_ref,
    pos_ref,
    w_in,
    w_own,
    perm,
    spread,
    beams_own,
    beams_in,
    hits,
    select,
    picked,
    rows_in,
    scored,
    half_out,
    block_out,
    half_left,
    half_right,
    block_left,
    block_right,
    total,
    returned,
    choose,
    columns,
    line,
    parent_out,
    parent_in,
    in_sem,
    w_sem,
    beam_send,
    beam_recv,
    z_send,
    z_recv,
    y_send,
    y_recv,
    fwd_send,
    fwd_recv,
    half_send,
    half_recv,
    block_send,
    block_recv,
    ret_send,
    ret_recv,
    parent_send,
    parent_recv,
):
    level = lax.axis_index("level")
    g = lax.axis_index("group")
    x = lax.axis_index("leaf")
    ny = ROWS_OF_CHIPS
    nz = groups // ny
    y, z = g // nz, g % nz
    right, left, across = (x + 1) % leaves, (x + leaves - 1) % leaves, (x + 2) % leaves
    fetched = 2 * (x % 2)
    other_two = 2 - fetched
    own_part = fetched + level
    beam_len, queries = beam_ref.shape
    feature, labels = w_ref.shape
    part = feature // leaves
    share = labels // leaves
    slots = groups * cap
    chunk = nz * cap
    half = chunk // 2

    copies = [
        pltpu.make_async_copy(src, dst, in_sem.at[n])
        for n, (src, dst) in enumerate(
            (
                (beam_hbm, beam_ref),
                (q_hbm, q_ref),
                (map_hbm, map_ref),
                (mask_hbm, mask_ref),
                (pos_hbm, pos_ref),
                (root_hbm, root_ref),
            )
        )
    ]
    for copy in copies:
        copy.start()
    weight_copy = pltpu.make_async_copy(w_ref, w_in, w_sem)
    weight_copy.start()

    barrier = pltpu.get_barrier_semaphore()

    def greet(o, carry):
        pl.semaphore_signal(
            barrier, inc=1, device_id={"group": (g + o) % groups}, device_id_type=MESH
        )
        return carry

    lax.fori_loop(1, groups, greet, 0)
    for other in (left, right):
        pl.semaphore_signal(barrier, inc=1, device_id={"leaf": other}, device_id_type=MESH)
    for n in range(1, leaves):
        pl.semaphore_signal(
            barrier,
            inc=1,
            device_id={"level": 1 - level, "leaf": (x + n) % leaves},
            device_id_type=MESH,
        )
    for n in range(nz):
        pl.semaphore_signal(
            barrier,
            inc=1,
            device_id={"level": 1 - level, "group": y * nz + (z + n) % nz},
            device_id_type=MESH,
        )
    for n in range(1, ny):
        pl.semaphore_signal(
            barrier,
            inc=1,
            device_id={"level": 1 - level, "group": ((y + n) % ny) * nz + z},
            device_id_type=MESH,
        )

    for copy in copies[:2]:
        copy.wait()
    beam = beam_ref[...]
    spread[0] = q_ref[:, pl.ds(pl.multiple_of(own_part * part, 128), part)]
    beams_own[...] = jnp.full_like(beams_own, -1)
    beams_own[:beam_len, :queries] = beam

    pl.semaphore_wait(barrier, groups - 1 + 2 + leaves - 1 + nz + ny - 1)

    def half_rows(which):
        return pl.ds(which * (queries // 2), queries // 2)

    def along_z(come, at, step, which=None):
        rows = pl.ds(0, queries) if which is None else half_rows(which)
        pltpu.make_async_remote_copy(
            src_ref=spread.at[come, rows],
            dst_ref=spread.at[at, rows],
            send_sem=z_send,
            recv_sem=z_recv.at[at],
            device_id={"group": y * nz + (z + nz + step) % nz},
            device_id_type=MESH,
        ).start()

    def from_z(at):
        wait_for(spread.at[at], z_recv.at[at])

    pltpu.make_async_copy(beams_own, beams_in.at[level * nz], beam_recv).start()
    for n in range(nz):
        at = 2 * n if n < nz // 2 else 2 * (nz - n) - 1
        for flip in range(2):
            if n or flip:
                pltpu.make_async_remote_copy(
                    src_ref=beams_own,
                    dst_ref=beams_in.at[level * nz + at],
                    send_sem=beam_send,
                    recv_sem=beam_recv,
                    device_id={
                        "level": (level + flip) % 2,
                        "group": y * nz + (z + n) % nz,
                    },
                    device_id_type=MESH,
                ).start()

    along_z(0, 2, 1)
    along_z(0, 1, -1)
    along_z(0, 4, 2)
    along_z(0, 3, -2)

    group_id = lax.broadcasted_iota(I32, (groups, queries), 0)
    hit = jnp.zeros((groups, queries), F32)
    for b in range(beam_len):
        hit = hit + (beam[b : b + 1, :] == group_id).astype(F32)
    earlier = (
        lax.broadcasted_iota(I32, (queries, queries), 0)
        < lax.broadcasted_iota(I32, (queries, queries), 1)
    ).astype(F32)
    rank = jnp.dot(hit.astype(BF16), earlier.astype(BF16), preferred_element_type=F32)
    place = group_id.astype(F32) * cap + rank
    slot = [
        jnp.sum(jnp.where(beam[b : b + 1, :] == group_id, place, 0.0), axis=0, keepdims=True)
        for b in range(beam_len)
    ]
    for copy in copies[2:]:
        copy.wait()
    tile, tall = 256, 1024
    mask_rows = feature // mask_ref.shape[0]

    def fill_perm(n, carry):
        at = pl.ds(pl.multiple_of(n * tile, tile), tile)
        column = lax.broadcasted_iota(I32, (tile, labels), 0) + n * tile
        perm[at, :] = (column == map_ref[...]).astype(F32).astype(BF16)
        return carry

    lax.fori_loop(0, labels // tile, fill_perm, 0)
    weight_copy.wait()

    def permute(n, carry):
        row = n // (labels // tile)
        at = pl.ds(pl.multiple_of((n % (labels // tile)) * tile, tile), tile)
        product = jnp.dot(
            w_in[pl.ds(pl.multiple_of(row * tall, tall), tall), :],
            perm[:, at],
            preferred_element_type=F32,
        )
        for m in range(tall // mask_rows):
            keep = mask_ref[row * (tall // mask_rows) + m].astype(F32)
            w_own[pl.ds(pl.multiple_of(row * tall + m * mask_rows, mask_rows), mask_rows), at] = (
                product[m * mask_rows : (m + 1) * mask_rows] * keep
            ).astype(BF16)
        return carry

    tiles = (feature // tall) * (labels // tile)
    def permute_part(n):
        lax.fori_loop(tiles * n // ny, tiles * (n + 1) // ny, permute, 0)

    permute_part(0)

    pos = pos_ref[...]
    parent_slot, parent_label = pos // labels, (pos % labels).astype(F32)
    root = root_ref[...].astype(F32)
    line[...] = jnp.zeros_like(line)
    for b in range(beam_len):
        line[b : b + 1, :queries] = slot[b]
        line[2 * beam_len + b : 2 * beam_len + b + 1, :queries] = parent_label[b : b + 1]
        line[3 * beam_len + b : 3 * beam_len + b + 1, :queries] = root[b : b + 1]
        slot_of = jnp.zeros((1, queries), F32)
        root_of = jnp.zeros((1, queries), F32)
        for s in range(beam_len):
            same = parent_slot[b : b + 1] == s
            slot_of = slot_of + jnp.where(same, slot[s], 0.0)
            root_of = root_of + jnp.where(same, root[s : s + 1], 0.0)
        line[beam_len + b : beam_len + b + 1, :queries] = slot_of
        line[4 * beam_len + b : 4 * beam_len + b + 1, :queries] = root_of
    columns[...] = jnp.transpose(line[...])
    across_slots = lax.broadcasted_iota(I32, (queries, slots), 1).astype(F32)
    for b in range(2 * beam_len):
        choose[b * queries : (b + 1) * queries, :] = (
            (columns[:queries, b : b + 1] == across_slots).astype(F32).astype(BF16)
        )

    wait_for(beams_in, beam_recv)
    eight = lax.broadcasted_iota(I32, (8, 128), 0)
    near_group = jnp.where(eight < ny, eight * nz + z, -2)

    def find_hits(n, carry):
        names = beams_in[n]
        found = jnp.zeros((8, 128), F32)
        for b in range(beam_len):
            found = found + (names[b : b + 1, :] == near_group).astype(F32)
        hits[pl.ds(pl.multiple_of(n * 8, 8), 8), :] = found
        return carry

    lax.fori_loop(0, 2 * nz, find_hits, 0)
    before = (
        lax.broadcasted_iota(I32, (128, 128), 0) < lax.broadcasted_iota(I32, (128, 128), 1)
    ).astype(F32)
    hits[...] = jnp.dot(
        hits[...].astype(BF16), before.astype(BF16), preferred_element_type=F32
    )
    near_slot = lax.broadcasted_iota(I32, (ny * cap, 128), 0).astype(F32)

    def make_select(n, carry):
        names = beams_in[n]
        place = eight.astype(F32) * cap + hits[pl.ds(pl.multiple_of(n * 8, 8), 8), :] + 1.0
        chosen = jnp.zeros((ny * cap, 128), F32)
        for b in range(beam_len):
            at = jnp.sum(
                jnp.where(names[b : b + 1, :] == near_group, place, 0.0), axis=0, keepdims=True
            )
            chosen = chosen + (at - 1.0 == near_slot).astype(F32)
        select[n % nz, pl.ds(pl.multiple_of((n // nz) * ny * cap, 16), ny * cap), :] = chosen.astype(
            BF16
        )
        return carry

    lax.fori_loop(0, 2 * nz, make_select, 0)

    blocks = cap // 8

    def slot_blocks(group):
        return pl.ds(group * blocks, blocks)

    def chunk_blocks(step):
        return pl.ds(step * (chunk // 8), chunk // 8)

    def distance_blocks(at):
        return pl.ds(at * (half // 8), half // 8)

    def pick(at):
        rows = jnp.dot(select[at, :, :queries], spread[at], preferred_element_type=F32)
        picked[at] = rows.astype(BF16).reshape(2, ny, blocks, 8, part)
        pltpu.make_async_copy(
            picked.at[at, level, y], rows_in.at[own_part, slot_blocks(at * ny + y)], y_recv.at[at // 2]
        ).start()
        for flip, step in ((0, 1), (0, 3), (1, 1), (1, 3), (1, 0), (0, 2), (1, 2)):
            to_level, to_row = (level + flip) % 2, (y + step) % ny
            pltpu.make_async_remote_copy(
                src_ref=picked.at[at, to_level, to_row],
                dst_ref=rows_in.at[own_part, slot_blocks(at * ny + y)],
                send_sem=y_send,
                recv_sem=y_recv.at[at // 2],
                device_id={"level": to_level, "group": to_row * nz + z},
                device_id_type=MESH,
            ).start()

    def to_leaf(src, dst, send, recv, other):
        pltpu.make_async_remote_copy(
            src_ref=src,
            dst_ref=dst,
            send_sem=send,
            recv_sem=recv,
            device_id={"leaf": other},
            device_id_type=MESH,
        ).start()

    def exchange(c):
        two = pl.ds(fetched, 2)
        wait_for(rows_in.at[two, chunk_blocks(c)], y_recv.at[c])
        for n, other in enumerate((right, left)):
            rows = rows_in.at[two, distance_blocks(2 * c + n)]
            to_leaf(rows, rows, fwd_send, fwd_recv.at[n, c], other)

    pick(0)
    for at in (1, 2):
        from_z(at)
        pick(at)
    from_z(4)
    along_z(4, 6, 1)
    along_z(4, 7, 2, 0)
    from_z(3)
    along_z(3, 5, -1)
    along_z(3, 7, -2, 1)
    pick(3)
    pick(4)
    permute_part(1)
    exchange(0)
    permute_part(2)
    for at in (5, 6):
        from_z(at)
        pick(at)
    exchange(1)
    from_z(7)
    pick(7)
    permute_part(3)

    def stage(t, carry):
        @pl.when(t < 2)
        def _():
            exchange(t + ny - 2)

        @pl.when(t < ny)
        def _():
            c = t
            two = pl.ds(other_two, 2)
            for n in range(2):
                wait_for(rows_in.at[two, distance_blocks(2 * c + n)], fwd_recv.at[n, c])

            logits = jnp.zeros((chunk, labels), F32)
            for p in range(leaves):
                logits = logits + jnp.dot(
                    rows_in[p, chunk_blocks(c)].reshape(chunk, part),
                    w_own[p * part : (p + 1) * part, :],
                    preferred_element_type=F32,
                )
            one_tree = jax.nn.sigmoid(logits)
            for j in range(leaves):
                scored[c, j] = one_tree[:, j * share : (j + 1) * share]
            half_out[c] = encode(scored[c, across])
            to_leaf(
                half_out.at[c, pl.ds(0, half)],
                half_left.at[c],
                half_send,
                half_recv.at[0, c],
                right,
            )
            to_leaf(
                half_out.at[c, pl.ds(half, half)],
                half_right.at[c],
                half_send,
                half_recv.at[1, c],
                left,
            )

        @pl.when((t >= 1) & (t < ny + 1))
        def _():
            c = t - 1
            wait_for(half_left.at[c], half_recv.at[0, c])
            block_out[c, 0, :half] = encode(scored[c, right, :half] + decode(half_left[c]))
            block_out[c, 0, half:] = encode(scored[c, right, half:])
            to_leaf(
                block_out.at[c, 0], block_left.at[c], block_send, block_recv.at[0, c], right
            )
            wait_for(half_right.at[c], half_recv.at[1, c])
            block_out[c, 1, :half] = encode(scored[c, left, :half])
            block_out[c, 1, half:] = encode(scored[c, left, half:] + decode(half_right[c]))
            to_leaf(
                block_out.at[c, 1], block_right.at[c], block_send, block_recv.at[1, c], left
            )

        @pl.when(t >= 2)
        def _():
            c = t - 2
            wait_for(block_left.at[c], block_recv.at[0, c])
            wait_for(block_right.at[c], block_recv.at[1, c])
            sums = scored[c, x] + (decode(block_left[c]) + decode(block_right[c]))
            total[c] = encode(sums.reshape(chunk // 8, 8, share))

            def send_back(n, carry):
                row = (y + n) % ny
                place = jnp.where(n < ny, z + nz - c, z + c + 1) % nz
                pltpu.make_async_remote_copy(
                    src_ref=total.at[c, slot_blocks((n // ny) * ny + row)],
                    dst_ref=returned.at[slot_blocks(g)],
                    send_sem=ret_send,
                    recv_sem=ret_recv,
                    device_id={"group": row * nz + place},
                    device_id_type=MESH,
                ).start()
                return carry

            @pl.when(c == 0)
            def _():
                pltpu.make_async_copy(
                    total.at[c, slot_blocks(y)], returned.at[slot_blocks(g)], ret_recv
                ).start()

            @pl.when(c > 0)
            def _():
                send_back(0, 0)

            lax.fori_loop(1, 2 * ny, send_back, 0)

        return carry

    lax.fori_loop(0, ny + 2, stage, 0)

    wait_for(returned, ret_recv)
    high, low = two_parts(decode(returned[...]).reshape(slots, share))
    entries = beam_len * queries

    def gather(at):
        chosen = choose[at, :]
        return jnp.dot(chosen, high, preferred_element_type=F32) + jnp.dot(
            chosen, low, preferred_element_type=F32
        )

    def to_level_one(other, carry):
        pltpu.make_async_remote_copy(
            src_ref=parent_out,
            dst_ref=parent_in.at[x],
            send_sem=parent_send,
            recv_sem=parent_recv,
            device_id={"level": 1, "leaf": other},
            device_id_type=MESH,
        ).start()
        return carry

    @pl.when(level == 0)
    def _():
        lane = lax.broadcasted_iota(I32, (queries, share), 1).astype(F32) + (x * share).astype(F32)
        wide = lax.broadcasted_iota(I32, (queries, 128), 1)
        sums = gather(slice(entries, 2 * entries))
        parents = jnp.zeros((queries, 128), F32)
        for b in range(beam_len):
            at_label = columns[:queries, 2 * beam_len + b : 2 * beam_len + b + 1] == lane
            mine = jnp.where(at_label, sums[b * queries : (b + 1) * queries], 0.0)
            value = jnp.sum(mine, axis=1, keepdims=True) * columns[
                :queries, 4 * beam_len + b : 4 * beam_len + b + 1
            ]
            parents = jnp.where(wide == b, value, parents)
        parent_out[...] = parents
        lax.fori_loop(0, leaves, to_level_one, 0)

    sums = gather(slice(0, entries))

    @pl.when(level == 0)
    def _():
        for b in range(beam_len):
            out_ref[b] = (
                sums[b * queries : (b + 1) * queries]
                * columns[:queries, 3 * beam_len + b : 3 * beam_len + b + 1]
            )

        wait_for(parent_in, parent_send)

    @pl.when(level == 1)
    def _():
        wait_for(parent_in, parent_recv)
        parents = parent_in[0]
        for n in range(1, leaves):
            parents = parents + parent_in[n]
        parents = (parents / leaves).astype(BF16).astype(F32)
        for b in range(beam_len):
            out_ref[b] = sums[b * queries : (b + 1) * queries] * parents[:, b : b + 1]

    wait_for(beams_in.at[pl.ds(0, 2 * nz - 1)], beam_send)
    wait_for(spread.at[pl.ds(0, nz - 1)], z_send)
    wait_for(picked.at[pl.ds(0, 7)], y_send)
    wait_for(rows_in.at[pl.ds(0, 2)], fwd_send)
    wait_for(half_out, half_send)
    wait_for(block_out, block_send)
    wait_for(returned.at[pl.ds(0, (groups - 1) * cap // 8)], ret_send)


def body(queries, weights, block_mask, label_map, beam_lists, root_score, parent_pos):
    groups, leaves = lax.axis_size("group"), lax.axis_size("leaf")
    rows, feature = queries.shape
    labels = weights.shape[4]
    beam_len = beam_lists.shape[2]
    cap = rows // QBLK * CAP
    slots = groups * cap
    ny = ROWS_OF_CHIPS
    nz = groups // ny
    chunk = slots // ny
    half = chunk // 2
    share = labels // leaves
    vmem = pl.BlockSpec(memory_space=pltpu.VMEM)
    dma = pltpu.SemaphoreType.DMA
    out = pl.pallas_call(
        functools.partial(kernel, groups, leaves, cap),
        out_shape=jax.ShapeDtypeStruct((beam_len, rows, share), F32),
        in_specs=[pl.BlockSpec(memory_space=pltpu.HBM)] * 7,
        out_specs=vmem,
        scratch_shapes=[
            pltpu.VMEM((rows, feature), BF16),
            pltpu.SMEM((block_mask.shape[3],), I32),
            pltpu.VMEM((1, labels), I32),
            pltpu.VMEM((beam_len, rows), I32),
            pltpu.VMEM((beam_len, rows), BF16),
            pltpu.VMEM((beam_len, rows), I32),
            pltpu.VMEM((feature, labels), BF16),
            pltpu.VMEM((feature, labels), BF16),
            pltpu.VMEM((labels, labels), BF16),
            pltpu.VMEM((nz, rows, feature // leaves), BF16),
            pltpu.VMEM((8, 128), I32),
            pltpu.VMEM((2 * nz, 8, 128), I32),
            pltpu.VMEM((16 * nz, 128), F32),
            pltpu.VMEM((nz, chunk, 128), BF16),
            pltpu.VMEM((nz, 2, ny, cap // 8, 8, feature // leaves), BF16),
            pltpu.VMEM((leaves, slots // 8, 8, feature // leaves), BF16),
            pltpu.VMEM((ny, leaves, chunk, share), F32),
            pltpu.VMEM((ny, chunk, share), I16),
            pltpu.VMEM((ny, 2, chunk, share), I16),
            pltpu.VMEM((ny, half, share), I16),
            pltpu.VMEM((ny, half, share), I16),
            pltpu.VMEM((ny, chunk, share), I16),
            pltpu.VMEM((ny, chunk, share), I16),
            pltpu.VMEM((ny, chunk // 8, 8, share), I16),
            pltpu.VMEM((slots // 8, 8, share), I16),
            pltpu.VMEM((2 * beam_len * rows, slots), BF16),
            pltpu.VMEM((128, 128), F32),
            pltpu.VMEM((128, 128), F32),
            pltpu.VMEM((rows, 128), F32),
            pltpu.VMEM((leaves, rows, 128), F32),
            dma((6,)),
            dma,
            dma,
            dma,
            dma,
            dma((nz,)),
            dma,
            dma((ny,)),
            dma,
            dma((2, ny)),
            dma,
            dma((2, ny)),
            dma,
            dma((2, ny)),
            dma,
            dma,
            dma,
            dma,
        ],
        compiler_params=pltpu.CompilerParams(
            collective_id=0, has_side_effects=True, vmem_limit_bytes=52 << 20
        ),
    )(
        *(
            pltpu.with_memory_space_constraint(operand, pltpu.HBM)
            for operand in (
                queries,
                weights[0, 0, 0],
                block_mask[0, 0, 0],
                label_map[0, 0],
                beam_lists[0].T,
                root_score.T,
                parent_pos.T,
            )
        )
    )
    return jnp.transpose(out, (1, 0, 2))[None]


def solution(mesh):
    in_specs = (
        P("group", None),
        P("level", "leaf", "group", None, None),
        P("level", "leaf", "group", None),
        P("level", "leaf", "group", None),
        P("level", "group", None),
        P("group", None),
        P("group", None),
    )
    out_specs = P("level", "group", None, "leaf")
    return jax.shard_map(body, mesh=mesh, in_specs=in_specs, out_specs=out_specs, check_vma=False)
```

```python
import functools

import jax
import jax.numpy as jnp
from jax import lax
from jax.experimental import pallas as pl
from jax.experimental.pallas import tpu as pltpu
from jax.sharding import PartitionSpec as P

QBLK = 32
CAP = 8
ROWS_OF_CHIPS = 4
MESH = pl.DeviceIdType.MESH
F32, BF16, I32, I16 = jnp.float32, jnp.bfloat16, jnp.int32, jnp.int16


def encode(value):
    octaves = jnp.log2(jnp.maximum(value, 2.0**-61))
    return jnp.round((octaves + 29.0) * 1024.0).astype(I32).astype(I16)


def decode(code):
    return jnp.exp2(code.astype(I32).astype(F32) * (1.0 / 1024.0) - 29.0)


def two_parts(value):
    high = value.astype(BF16)
    return high, (value - high.astype(F32)).astype(BF16)


def wait_for(ref, sem):
    pltpu.make_async_copy(ref, ref, sem).wait()


def kernel(
    groups,
    leaves,
    cap,
    q_hbm,
    w_ref,
    mask_hbm,
    map_hbm,
    beam_hbm,
    root_hbm,
    pos_hbm,
    out_ref,
    q_ref,
    mask_ref,
    map_ref,
    beam_ref,
    root_ref,
    pos_ref,
    w_in,
    w_own,
    perm,
    spread,
    beams_own,
    beams_in,
    hits,
    select,
    picked,
    rows_in,
    scored,
    half_out,
    block_out,
    half_left,
    half_right,
    block_left,
    block_right,
    total,
    returned,
    choose,
    columns,
    line,
    parent_out,
    parent_in,
    in_sem,
    w_sem,
    beam_send,
    beam_recv,
    z_send,
    z_recv,
    y_send,
    y_recv,
    fwd_send,
    fwd_recv,
    half_send,
    half_recv,
    block_send,
    block_recv,
    ret_send,
    ret_recv,
    parent_send,
    parent_recv,
):
    level = lax.axis_index("level")
    g = lax.axis_index("group")
    x = lax.axis_index("leaf")
    ny = ROWS_OF_CHIPS
    nz = groups // ny
    y, z = g // nz, g % nz
    right, left, across = (x + 1) % leaves, (x + leaves - 1) % leaves, (x + 2) % leaves
    fetched = 2 * (x % 2)
    other_two = 2 - fetched
    own_part = fetched + level
    beam_len, queries = beam_ref.shape
    feature, labels = w_ref.shape
    part = feature // leaves
    share = labels // leaves
    slots = groups * cap
    chunk = nz * cap
    half = chunk // 2

    copies = [
        pltpu.make_async_copy(src, dst, in_sem.at[n])
        for n, (src, dst) in enumerate(
            (
                (beam_hbm, beam_ref),
                (q_hbm, q_ref),
                (map_hbm, map_ref),
                (mask_hbm, mask_ref),
                (pos_hbm, pos_ref),
                (root_hbm, root_ref),
            )
        )
    ]
    for copy in copies:
        copy.start()
    weight_copy = pltpu.make_async_copy(w_ref, w_in, w_sem)
    weight_copy.start()

    barrier = pltpu.get_barrier_semaphore()

    def greet(o, carry):
        pl.semaphore_signal(
            barrier, inc=1, device_id={"group": (g + o) % groups}, device_id_type=MESH
        )
        return carry

    lax.fori_loop(1, groups, greet, 0)
    for other in (left, right):
        pl.semaphore_signal(barrier, inc=1, device_id={"leaf": other}, device_id_type=MESH)
    for n in range(1, leaves):
        pl.semaphore_signal(
            barrier,
            inc=1,
            device_id={"level": 1 - level, "leaf": (x + n) % leaves},
            device_id_type=MESH,
        )
    for n in range(nz):
        pl.semaphore_signal(
            barrier,
            inc=1,
            device_id={"level": 1 - level, "group": y * nz + (z + n) % nz},
            device_id_type=MESH,
        )
    for n in range(1, ny):
        pl.semaphore_signal(
            barrier,
            inc=1,
            device_id={"level": 1 - level, "group": ((y + n) % ny) * nz + z},
            device_id_type=MESH,
        )

    for copy in copies[:2]:
        copy.wait()
    beam = beam_ref[...]
    spread[0] = q_ref[:, pl.ds(pl.multiple_of(own_part * part, 128), part)]
    beams_own[...] = jnp.full_like(beams_own, -1)
    beams_own[:beam_len, :queries] = beam

    pl.semaphore_wait(barrier, groups - 1 + 2 + leaves - 1 + nz + ny - 1)

    def half_rows(which):
        return pl.ds(which * (queries // 2), queries // 2)

    def along_z(come, at, step, which=None):
        rows = pl.ds(0, queries) if which is None else half_rows(which)
        pltpu.make_async_remote_copy(
            src_ref=spread.at[come, rows],
            dst_ref=spread.at[at, rows],
            send_sem=z_send,
            recv_sem=z_recv.at[at],
            device_id={"group": y * nz + (z + nz + step) % nz},
            device_id_type=MESH,
        ).start()

    def from_z(at):
        wait_for(spread.at[at], z_recv.at[at])

    pltpu.make_async_copy(beams_own, beams_in.at[level * nz], beam_recv).start()
    for n in range(nz):
        at = 2 * n if n < nz // 2 else 2 * (nz - n) - 1
        for flip in range(2):
            if n or flip:
                pltpu.make_async_remote_copy(
                    src_ref=beams_own,
                    dst_ref=beams_in.at[level * nz + at],
                    send_sem=beam_send,
                    recv_sem=beam_recv,
                    device_id={
                        "level": (level + flip) % 2,
                        "group": y * nz + (z + n) % nz,
                    },
                    device_id_type=MESH,
                ).start()

    along_z(0, 2, 1)
    along_z(0, 1, -1)
    along_z(0, 4, 2)
    along_z(0, 3, -2)

    group_id = lax.broadcasted_iota(I32, (groups, queries), 0)
    hit = jnp.zeros((groups, queries), F32)
    for b in range(beam_len):
        hit = hit + (beam[b : b + 1, :] == group_id).astype(F32)
    earlier = (
        lax.broadcasted_iota(I32, (queries, queries), 0)
        < lax.broadcasted_iota(I32, (queries, queries), 1)
    ).astype(F32)
    rank = jnp.dot(hit.astype(BF16), earlier.astype(BF16), preferred_element_type=F32)
    place = group_id.astype(F32) * cap + rank
    slot = [
        jnp.sum(jnp.where(beam[b : b + 1, :] == group_id, place, 0.0), axis=0, keepdims=True)
        for b in range(beam_len)
    ]
    for copy in copies[2:]:
        copy.wait()
    tile, tall = 256, 2048
    mask_rows = feature // mask_ref.shape[0]

    def fill_perm(n, carry):
        at = pl.ds(pl.multiple_of(n * tile, tile), tile)
        column = lax.broadcasted_iota(I32, (tile, labels), 0) + n * tile
        perm[at, :] = (column == map_ref[...]).astype(F32).astype(BF16)
        return carry

    lax.fori_loop(0, labels // tile, fill_perm, 0)
    weight_copy.wait()

    def permute(n, carry):
        row = n // (labels // tile)
        at = pl.ds(pl.multiple_of((n % (labels // tile)) * tile, tile), tile)
        product = jnp.dot(
            w_in[pl.ds(pl.multiple_of(row * tall, tall), tall), :],
            perm[:, at],
            preferred_element_type=F32,
        )
        for m in range(tall // mask_rows):
            keep = mask_ref[row * (tall // mask_rows) + m].astype(F32)
            w_own[pl.ds(pl.multiple_of(row * tall + m * mask_rows, mask_rows), mask_rows), at] = (
                product[m * mask_rows : (m + 1) * mask_rows] * keep
            ).astype(BF16)
        return carry

    tiles = (feature // tall) * (labels // tile)
    def permute_part(n):
        lax.fori_loop(tiles * n // ny, tiles * (n + 1) // ny, permute, 0)

    permute_part(0)

    pos = pos_ref[...]
    parent_slot, parent_label = pos // labels, (pos % labels).astype(F32)
    root = root_ref[...].astype(F32)
    line[...] = jnp.zeros_like(line)
    for b in range(beam_len):
        line[b : b + 1, :queries] = slot[b]
        line[2 * beam_len + b : 2 * beam_len + b + 1, :queries] = parent_label[b : b + 1]
        line[3 * beam_len + b : 3 * beam_len + b + 1, :queries] = root[b : b + 1]
        slot_of = jnp.zeros((1, queries), F32)
        root_of = jnp.zeros((1, queries), F32)
        for s in range(beam_len):
            same = parent_slot[b : b + 1] == s
            slot_of = slot_of + jnp.where(same, slot[s], 0.0)
            root_of = root_of + jnp.where(same, root[s : s + 1], 0.0)
        line[beam_len + b : beam_len + b + 1, :queries] = slot_of
        line[4 * beam_len + b : 4 * beam_len + b + 1, :queries] = root_of
    columns[...] = jnp.transpose(line[...])
    across_slots = lax.broadcasted_iota(I32, (queries, slots), 1).astype(F32)
    for b in range(2 * beam_len):
        choose[b * queries : (b + 1) * queries, :] = (
            (columns[:queries, b : b + 1] == across_slots).astype(F32).astype(BF16)
        )

    wait_for(beams_in, beam_recv)
    eight = lax.broadcasted_iota(I32, (8, 128), 0)
    near_group = jnp.where(eight < ny, eight * nz + z, -2)

    def find_hits(n, carry):
        names = beams_in[n]
        found = jnp.zeros((8, 128), F32)
        for b in range(beam_len):
            found = found + (names[b : b + 1, :] == near_group).astype(F32)
        hits[pl.ds(pl.multiple_of(n * 8, 8), 8), :] = found
        return carry

    lax.fori_loop(0, 2 * nz, find_hits, 0)
    before = (
        lax.broadcasted_iota(I32, (128, 128), 0) < lax.broadcasted_iota(I32, (128, 128), 1)
    ).astype(F32)
    hits[...] = jnp.dot(
        hits[...].astype(BF16), before.astype(BF16), preferred_element_type=F32
    )
    near_slot = lax.broadcasted_iota(I32, (ny * cap, 128), 0).astype(F32)

    def make_select(n, carry):
        names = beams_in[n]
        place = eight.astype(F32) * cap + hits[pl.ds(pl.multiple_of(n * 8, 8), 8), :] + 1.0
        chosen = jnp.zeros((ny * cap, 128), F32)
        for b in range(beam_len):
            at = jnp.sum(
                jnp.where(names[b : b + 1, :] == near_group, place, 0.0), axis=0, keepdims=True
            )
            chosen = chosen + (at - 1.0 == near_slot).astype(F32)
        select[n % nz, pl.ds(pl.multiple_of((n // nz) * ny * cap, 16), ny * cap), :] = chosen.astype(
            BF16
        )
        return carry

    lax.fori_loop(0, 2 * nz, make_select, 0)

    blocks = cap // 8

    def slot_blocks(group):
        return pl.ds(group * blocks, blocks)

    def chunk_blocks(step):
        return pl.ds(step * (chunk // 8), chunk // 8)

    def distance_blocks(at):
        return pl.ds(at * (half // 8), half // 8)

    def pick(at):
        rows = jnp.dot(select[at, :, :queries], spread[at], preferred_element_type=F32)
        picked[at] = rows.astype(BF16).reshape(2, ny, blocks, 8, part)
        pltpu.make_async_copy(
            picked.at[at, level, y], rows_in.at[own_part, slot_blocks(at * ny + y)], y_recv.at[at // 2]
        ).start()
        for flip, step in ((0, 1), (0, 3), (1, 1), (1, 3), (1, 0), (0, 2), (1, 2)):
            to_level, to_row = (level + flip) % 2, (y + step) % ny
            pltpu.make_async_remote_copy(
                src_ref=picked.at[at, to_level, to_row],
                dst_ref=rows_in.at[own_part, slot_blocks(at * ny + y)],
                send_sem=y_send,
                recv_sem=y_recv.at[at // 2],
                device_id={"level": to_level, "group": to_row * nz + z},
                device_id_type=MESH,
            ).start()

    def to_leaf(src, dst, send, recv, other):
        pltpu.make_async_remote_copy(
            src_ref=src,
            dst_ref=dst,
            send_sem=send,
            recv_sem=recv,
            device_id={"leaf": other},
            device_id_type=MESH,
        ).start()

    def exchange(c):
        two = pl.ds(fetched, 2)
        wait_for(rows_in.at[two, chunk_blocks(c)], y_recv.at[c])
        for n, other in enumerate((right, left)):
            rows = rows_in.at[two, distance_blocks(2 * c + n)]
            to_leaf(rows, rows, fwd_send, fwd_recv.at[n, c], other)

    pick(0)
    for at in (1, 2):
        from_z(at)
        pick(at)
    from_z(4)
    along_z(4, 6, 1)
    along_z(4, 7, 2, 0)
    from_z(3)
    along_z(3, 5, -1)
    along_z(3, 7, -2, 1)
    pick(3)
    pick(4)
    permute_part(1)
    exchange(0)
    permute_part(2)
    for at in (5, 6):
        from_z(at)
        pick(at)
    exchange(1)
    from_z(7)
    pick(7)
    permute_part(3)

    def stage(t, carry):
        @pl.when(t < 2)
        def _():
            exchange(t + ny - 2)

        @pl.when(t < ny)
        def _():
            c = t
            two = pl.ds(other_two, 2)
            for n in range(2):
                wait_for(rows_in.at[two, distance_blocks(2 * c + n)], fwd_recv.at[n, c])

            logits = jnp.zeros((chunk, labels), F32)
            for p in range(leaves):
                logits = logits + jnp.dot(
                    rows_in[p, chunk_blocks(c)].reshape(chunk, part),
                    w_own[p * part : (p + 1) * part, :],
                    preferred_element_type=F32,
                )
            one_tree = jax.nn.sigmoid(logits)
            for j in range(leaves):
                scored[c, j] = one_tree[:, j * share : (j + 1) * share]
            half_out[c] = encode(scored[c, across])
            to_leaf(
                half_out.at[c, pl.ds(0, half)],
                half_left.at[c],
                half_send,
                half_recv.at[0, c],
                right,
            )
            to_leaf(
                half_out.at[c, pl.ds(half, half)],
                half_right.at[c],
                half_send,
                half_recv.at[1, c],
                left,
            )

        @pl.when((t >= 1) & (t < ny + 1))
        def _():
            c = t - 1
            wait_for(half_left.at[c], half_recv.at[0, c])
            block_out[c, 0, :half] = encode(scored[c, right, :half] + decode(half_left[c]))
            block_out[c, 0, half:] = encode(scored[c, right, half:])
            to_leaf(
                block_out.at[c, 0], block_left.at[c], block_send, block_recv.at[0, c], right
            )
            wait_for(half_right.at[c], half_recv.at[1, c])
            block_out[c, 1, :half] = encode(scored[c, left, :half])
            block_out[c, 1, half:] = encode(scored[c, left, half:] + decode(half_right[c]))
            to_leaf(
                block_out.at[c, 1], block_right.at[c], block_send, block_recv.at[1, c], left
            )

        @pl.when(t >= 2)
        def _():
            c = t - 2
            wait_for(block_left.at[c], block_recv.at[0, c])
            wait_for(block_right.at[c], block_recv.at[1, c])
            sums = scored[c, x] + (decode(block_left[c]) + decode(block_right[c]))
            total[c] = encode(sums.reshape(chunk // 8, 8, share))

            def send_back(n, carry):
                row = (y + n) % ny
                place = jnp.where(n < ny, z + nz - c, z + c + 1) % nz
                pltpu.make_async_remote_copy(
                    src_ref=total.at[c, slot_blocks((n // ny) * ny + row)],
                    dst_ref=returned.at[slot_blocks(g)],
                    send_sem=ret_send,
                    recv_sem=ret_recv,
                    device_id={"group": row * nz + place},
                    device_id_type=MESH,
                ).start()
                return carry

            @pl.when(c == 0)
            def _():
                pltpu.make_async_copy(
                    total.at[c, slot_blocks(y)], returned.at[slot_blocks(g)], ret_recv
                ).start()

            @pl.when(c > 0)
            def _():
                send_back(0, 0)

            lax.fori_loop(1, 2 * ny, send_back, 0)

        return carry

    lax.fori_loop(0, ny + 2, stage, 0)

    wait_for(returned, ret_recv)
    high, low = two_parts(decode(returned[...]).reshape(slots, share))
    entries = beam_len * queries

    def gather(at):
        chosen = choose[at, :]
        return jnp.dot(chosen, high, preferred_element_type=F32) + jnp.dot(
            chosen, low, preferred_element_type=F32
        )

    def to_level_one(other, carry):
        pltpu.make_async_remote_copy(
            src_ref=parent_out,
            dst_ref=parent_in.at[x],
            send_sem=parent_send,
            recv_sem=parent_recv,
            device_id={"level": 1, "leaf": other},
            device_id_type=MESH,
        ).start()
        return carry

    @pl.when(level == 0)
    def _():
        lane = lax.broadcasted_iota(I32, (queries, share), 1).astype(F32) + (x * share).astype(F32)
        wide = lax.broadcasted_iota(I32, (queries, 128), 1)
        sums = gather(slice(entries, 2 * entries))
        parents = jnp.zeros((queries, 128), F32)
        for b in range(beam_len):
            at_label = columns[:queries, 2 * beam_len + b : 2 * beam_len + b + 1] == lane
            mine = jnp.where(at_label, sums[b * queries : (b + 1) * queries], 0.0)
            value = jnp.sum(mine, axis=1, keepdims=True) * columns[
                :queries, 4 * beam_len + b : 4 * beam_len + b + 1
            ]
            parents = jnp.where(wide == b, value, parents)
        parent_out[...] = parents
        lax.fori_loop(0, leaves, to_level_one, 0)

    sums = gather(slice(0, entries))

    @pl.when(level == 0)
    def _():
        for b in range(beam_len):
            out_ref[b] = (
                sums[b * queries : (b + 1) * queries]
                * columns[:queries, 3 * beam_len + b : 3 * beam_len + b + 1]
            )

        wait_for(parent_in, parent_send)

    @pl.when(level == 1)
    def _():
        wait_for(parent_in, parent_recv)
        parents = parent_in[0]
        for n in range(1, leaves):
            parents = parents + parent_in[n]
        parents = (parents / leaves).astype(BF16).astype(F32)
        for b in range(beam_len):
            out_ref[b] = sums[b * queries : (b + 1) * queries] * parents[:, b : b + 1]

    wait_for(beams_in.at[pl.ds(0, 2 * nz - 1)], beam_send)
    wait_for(spread.at[pl.ds(0, nz - 1)], z_send)
    wait_for(picked.at[pl.ds(0, 7)], y_send)
    wait_for(rows_in.at[pl.ds(0, 2)], fwd_send)
    wait_for(half_out, half_send)
    wait_for(block_out, block_send)
    wait_for(returned.at[pl.ds(0, (groups - 1) * cap // 8)], ret_send)


def body(queries, weights, block_mask, label_map, beam_lists, root_score, parent_pos):
    groups, leaves = lax.axis_size("group"), lax.axis_size("leaf")
    rows, feature = queries.shape
    labels = weights.shape[4]
    beam_len = beam_lists.shape[2]
    cap = rows // QBLK * CAP
    slots = groups * cap
    ny = ROWS_OF_CHIPS
    nz = groups // ny
    chunk = slots // ny
    half = chunk // 2
    share = labels // leaves
    vmem = pl.BlockSpec(memory_space=pltpu.VMEM)
    dma = pltpu.SemaphoreType.DMA
    out = pl.pallas_call(
        functools.partial(kernel, groups, leaves, cap),
        out_shape=jax.ShapeDtypeStruct((beam_len, rows, share), F32),
        in_specs=[pl.BlockSpec(memory_space=pltpu.HBM)] * 7,
        out_specs=vmem,
        scratch_shapes=[
            pltpu.VMEM((rows, feature), BF16),
            pltpu.SMEM((block_mask.shape[3],), I32),
            pltpu.VMEM((1, labels), I32),
            pltpu.VMEM((beam_len, rows), I32),
            pltpu.VMEM((beam_len, rows), BF16),
            pltpu.VMEM((beam_len, rows), I32),
            pltpu.VMEM((feature, labels), BF16),
            pltpu.VMEM((feature, labels), BF16),
            pltpu.VMEM((labels, labels), BF16),
            pltpu.VMEM((nz, rows, feature // leaves), BF16),
            pltpu.VMEM((8, 128), I32),
            pltpu.VMEM((2 * nz, 8, 128), I32),
            pltpu.VMEM((16 * nz, 128), F32),
            pltpu.VMEM((nz, chunk, 128), BF16),
            pltpu.VMEM((nz, 2, ny, cap // 8, 8, feature // leaves), BF16),
            pltpu.VMEM((leaves, slots // 8, 8, feature // leaves), BF16),
            pltpu.VMEM((ny, leaves, chunk, share), F32),
            pltpu.VMEM((ny, chunk, share), I16),
            pltpu.VMEM((ny, 2, chunk, share), I16),
            pltpu.VMEM((ny, half, share), I16),
            pltpu.VMEM((ny, half, share), I16),
            pltpu.VMEM((ny, chunk, share), I16),
            pltpu.VMEM((ny, chunk, share), I16),
            pltpu.VMEM((ny, chunk // 8, 8, share), I16),
            pltpu.VMEM((slots // 8, 8, share), I16),
            pltpu.VMEM((2 * beam_len * rows, slots), BF16),
            pltpu.VMEM((128, 128), F32),
            pltpu.VMEM((128, 128), F32),
            pltpu.VMEM((rows, 128), F32),
            pltpu.VMEM((leaves, rows, 128), F32),
            dma((6,)),
            dma,
            dma,
            dma,
            dma,
            dma((nz,)),
            dma,
            dma((ny,)),
            dma,
            dma((2, ny)),
            dma,
            dma((2, ny)),
            dma,
            dma((2, ny)),
            dma,
            dma,
            dma,
            dma,
        ],
        compiler_params=pltpu.CompilerParams(
            collective_id=0, has_side_effects=True, vmem_limit_bytes=52 << 20
        ),
    )(
        *(
            pltpu.with_memory_space_constraint(operand, pltpu.HBM)
            for operand in (
                queries,
                weights[0, 0, 0],
                block_mask[0, 0, 0],
                label_map[0, 0],
                beam_lists[0].T,
                root_score.T,
                parent_pos.T,
            )
        )
    )
    return jnp.transpose(out, (1, 0, 2))[None]


def solution(mesh):
    in_specs = (
        P("group", None),
        P("level", "leaf", "group", None, None),
        P("level", "leaf", "group", None),
        P("level", "leaf", "group", None),
        P("level", "group", None),
        P("group", None),
        P("group", None),
    )
    out_specs = P("level", "group", None, "leaf")
    return jax.shard_map(body, mesh=mesh, in_specs=in_specs, out_specs=out_specs, check_vma=False)
```
